32 devices in a mesh: dp: 8 (over y, x, core), mp: 4 (over z).
Axes of the slice: x: 2, y: 2, z: 4, core: 2. Of those that a mesh axis runs over, the one named last changes fastest.
Arguments:
- series: bfloat16 [8, 512, 16, 256], P('dp', 'mp'), may hold values from -6 to 6
- upstream_grad: bfloat16 [8, 512, 16, 256], P('dp', None, 'mp'), may hold values from -3 to 3
- time_weights: bfloat16 [4, 256, 256], replicated, may hold values from -0.375 to 0.375
- channel_weights: bfloat16 [4, 256, 256], replicated, may hold values from -0.375 to 0.375
- neighbors: int32 [4, 3], replicated, may hold values from 0 to 3, as said below
Outputs:
- mixed_series: bfloat16 [8, 512, 16, 256], P('dp', None, 'mp')
- series_grad: bfloat16 [8, 512, 16, 256], P('dp', 'mp')
- time_grads: float32 [4, 256, 256], P(None, 'mp')
- channel_grads: float32 [4, 256, 256], P(None, 'mp')
The draws below stay inside these ranges and needn't reach their ends.
Inputs may be any that keep to these rules, and one draw needn't show every extreme that they name: `neighbors`: row b names 3 different blocks; its first entry is b.
All inputs are finite; a program needn't handle non-finite values.
Results may differ from the reference program's by a relative error of at most 0.025.
Values may be sent and summed in bfloat16 or wider, within the bound.
A program may use at most 192 MiB of HBM per device.

```python
import jax
import jax.numpy as jnp
from jax import lax

D = 256
HEADS = 4
NBR = 3
L = 16
B = 8
C = 512
BLOCKS = 4


def draw_neighbors(key, part):
    attention_logits = jax.random.randint(key, (BLOCKS, BLOCKS), 0, 4096, dtype=jnp.int32)
    columns = jnp.arange(BLOCKS, dtype=jnp.int32)
    attention_logits = attention_logits * BLOCKS + columns[None, :]
    attention_logits = jnp.where(columns[None, :] == columns[:, None], jnp.int32(1 << 30), attention_logits)
    order = jnp.argsort(attention_logits, axis=1, stable=True).astype(jnp.int32)
    return jnp.concatenate([columns[:, None], order[:, :NBR - 1]], axis=1).astype(jnp.int32)


def level_of(key, shape, split, smallest, largest):
    gain = 1.0
    for axis_at, blocks in split:
        steps = jax.random.uniform(jax.random.fold_in(jax.random.fold_in(key, 6), axis_at), (blocks,), jnp.float32, smallest / len(split), largest / len(split))
        gain = gain * jnp.repeat(jnp.exp(steps), shape[axis_at] // blocks).reshape((-1,) + (1,) * (len(shape) - 1 - axis_at))
    return gain


def normal_values(rng, extent, spread, limit, cuts=(), held_as=jnp.bfloat16):
    entries = spread * jax.random.normal(rng, extent, jnp.float32)
    if cuts:
        entries = entries * level_of(rng, extent, cuts, -0.22, 0.18)
    return jnp.clip(entries, -limit, limit).astype(held_as)


def setup_inputs(seed: int = 0) -> dict:
    key_list = jax.random.split(jax.random.key(seed), 6)
    return {
        "series": normal_values(key_list[0], (B, C, L, D), 1.0, 6.0, ((0, 8), (1, 4))),
        "upstream_grad": normal_values(key_list[1], (B, C, L, D), 0.5, 3.0, ((0, 8), (2, 4))),
        "time_weights": normal_values(key_list[2], (4, D, D), D ** -0.5, 0.375),
        "channel_weights": normal_values(key_list[3], (4, D, D), D ** -0.5, 0.375),
        "neighbors": draw_neighbors(jax.random.fold_in(key_list[5], 71), 0),
    }


EPS = 1e-06
LOGIT_SCALE = 0.25

def cast_to_single_float(values):
    return values.astype(jnp.float32)

def cast_to_brain_float(values):
    return lax.optimization_barrier(values.astype(jnp.bfloat16))

def row_norm(inputs):
    return inputs * lax.rsqrt(lax.optimization_barrier(jnp.mean(inputs * inputs, axis=-1, keepdims=True)) + EPS)

def head_norm(inputs):
    shaped = inputs.reshape(inputs.shape[:-1] + (HEADS, inputs.shape[-1] // HEADS))
    return row_norm(shaped).reshape(inputs.shape)

def project(normed, weights):
    raw_query = jnp.dot(normed, weights[0], preferred_element_type=jnp.float32)
    raw_key = jnp.dot(normed, weights[1], preferred_element_type=jnp.float32)
    value_rows = cast_to_brain_float(jnp.dot(normed, weights[2], preferred_element_type=jnp.float32))
    query_rows = cast_to_brain_float(head_norm(raw_query))
    key_rows = cast_to_brain_float(head_norm(raw_key))
    return (raw_query, raw_key, query_rows, key_rows, value_rows)

def project_back(normed, raw_query, raw_key, query_grad, key_grad, value_grad, weights):
    query_back = cast_to_brain_float(jax.vjp(head_norm, raw_query)[1](query_grad)[0])
    key_back = cast_to_brain_float(jax.vjp(head_norm, raw_key)[1](key_grad)[0])
    value_back = cast_to_brain_float(value_grad)
    weight_grads = [jnp.dot(normed.T, back_rows, preferred_element_type=jnp.float32) for back_rows in (query_back, key_back, value_back)]
    normed_grad = jnp.dot(query_back, weights[0].T, preferred_element_type=jnp.float32)
    normed_grad = normed_grad + jnp.dot(key_back, weights[1].T, preferred_element_type=jnp.float32)
    normed_grad = normed_grad + jnp.dot(value_back, weights[2].T, preferred_element_type=jnp.float32)
    return (normed_grad, weight_grads)

def attend_time(query_heads, key_heads, value_heads):
    attention_logits = LOGIT_SCALE * jnp.einsum('clhe,cmhe->hlmc', cast_to_single_float(query_heads), cast_to_single_float(key_heads))
    exponent = jnp.exp(attention_logits)
    attention_layer = exponent / lax.optimization_barrier(jnp.sum(exponent, axis=2, keepdims=True))
    weights_brain_float = cast_to_brain_float(attention_layer)
    mixed_heads = jnp.einsum('hlmc,cmhe->clhe', cast_to_single_float(weights_brain_float), cast_to_single_float(value_heads))
    return (cast_to_brain_float(mixed_heads), attention_layer)

def revert_time(query_heads, key_heads, value_heads, attention_layer, grad_heads):
    weights_brain_float = cast_to_brain_float(attention_layer)
    attention_gradient = jnp.einsum('clhe,cmhe->hlmc', cast_to_single_float(grad_heads), cast_to_single_float(value_heads))
    row_delta = lax.optimization_barrier(jnp.sum(attention_layer * attention_gradient, axis=2, keepdims=True))
    logit_gradient = cast_to_brain_float(LOGIT_SCALE * attention_layer * (attention_gradient - row_delta))
    query_grad = jnp.einsum('hlmc,cmhe->clhe', cast_to_single_float(logit_gradient), cast_to_single_float(key_heads))
    key_grad = jnp.einsum('hlmc,clhe->cmhe', cast_to_single_float(logit_gradient), cast_to_single_float(query_heads))
    value_grad = jnp.einsum('hlmc,clhe->cmhe', cast_to_single_float(weights_brain_float), cast_to_single_float(grad_heads))
    return (query_grad, key_grad, value_grad)

def forward_time(series_rows, weights):
    channel_count, length, features = series_rows.shape
    total_rows = channel_count * length
    normed = cast_to_brain_float(row_norm(cast_to_single_float(series_rows))).reshape(total_rows, features)
    raw_query, raw_key, query_rows, key_rows, value_rows = project(normed, weights)
    shaped = (channel_count, length, HEADS, features // HEADS)
    mixed_heads, attention_layer = attend_time(query_rows.reshape(shaped), key_rows.reshape(shaped), value_rows.reshape(shaped))
    mixed_flat = mixed_heads.reshape(total_rows, features)
    branch = jnp.dot(mixed_flat, weights[3], preferred_element_type=jnp.float32).reshape(series_rows.shape)
    stream = cast_to_brain_float(cast_to_single_float(series_rows) + branch)
    return (stream, (normed, raw_query, raw_key, query_rows, key_rows, value_rows, mixed_flat, attention_layer))

def backward_time(series_rows, stored, stream_grad, weights):
    normed, raw_query, raw_key, query_rows, key_rows, value_rows, mixed_flat, attention_layer = stored
    channel_count, length, features = series_rows.shape
    total_rows = channel_count * length
    shaped = (channel_count, length, HEADS, features // HEADS)
    grad_flat = stream_grad.reshape(total_rows, features)
    out_grad = jnp.dot(mixed_flat.T, grad_flat, preferred_element_type=jnp.float32)
    mixed_grad = cast_to_brain_float(jnp.dot(grad_flat, weights[3].T, preferred_element_type=jnp.float32))
    query_grad, key_grad, value_grad = revert_time(query_rows.reshape(shaped), key_rows.reshape(shaped), value_rows.reshape(shaped), attention_layer, mixed_grad.reshape(shaped))
    normed_grad, weight_grads = project_back(normed, raw_query, raw_key, query_grad.reshape(total_rows, features), key_grad.reshape(total_rows, features), value_grad.reshape(total_rows, features), weights)
    norm_back = jax.vjp(row_norm, cast_to_single_float(series_rows))[1]
    series_grad = cast_to_brain_float(cast_to_single_float(stream_grad) + norm_back(normed_grad.reshape(series_rows.shape))[0])
    return (series_grad, jnp.stack(weight_grads + [out_grad]))

def near_blocks(source_rows, neighbors):
    block_list = neighbors.shape[0]
    shaped = source_rows.reshape(block_list, source_rows.shape[0] // block_list, source_rows.shape[1])
    return shaped[neighbors].reshape(block_list, -1, source_rows.shape[1])

def attend_channels(query_rows, key_rows, value_rows, neighbors):
    block_list = neighbors.shape[0]
    features = query_rows.shape[1]
    head_width = features // HEADS
    query_blocks = query_rows.reshape(block_list, -1, features)
    key_near = near_blocks(key_rows, neighbors)
    value_near = near_blocks(value_rows, neighbors)
    per_head_output = []
    for head_number in range(HEADS):
        first_col = head_number * head_width
        single_query_head = query_blocks[:, :, first_col:first_col + head_width]
        single_key_head = key_near[:, :, first_col:first_col + head_width]
        single_value_head = value_near[:, :, first_col:first_col + head_width]
        attention_logits = LOGIT_SCALE * jnp.einsum('fdr,fwr->fdw', cast_to_single_float(single_query_head), cast_to_single_float(single_key_head))
        exponent = jnp.exp(attention_logits)
        attention_layer = exponent / lax.optimization_barrier(jnp.sum(exponent, axis=2, keepdims=True))
        per_head_output.append(jnp.einsum('xlj,xjr->xlr', cast_to_single_float(cast_to_brain_float(attention_layer)), cast_to_single_float(single_value_head)))
    return cast_to_brain_float(jnp.concatenate(per_head_output, axis=2).reshape(query_rows.shape))

def join_heads(head_parts, shape):
    return jnp.concatenate(head_parts, axis=2).reshape(shape)

def revert_channels(query_rows, key_rows, value_rows, neighbors, mixed_grad):
    block_list, neighbor_count = neighbors.shape
    features = query_rows.shape[1]
    head_width = features // HEADS
    block_length = query_rows.shape[0] // block_list
    onehot = (neighbors.reshape(-1)[:, None] == jnp.arange(block_list, dtype=jnp.int32)[None, :]).astype(jnp.float32)
    query_blocks = query_rows.reshape(block_list, -1, features)
    grad_blocks = mixed_grad.reshape(block_list, -1, features)
    key_near = near_blocks(key_rows, neighbors)
    value_near = near_blocks(value_rows, neighbors)
    query_pieces_list, key_parts, value_parts = ([], [], [])
    for head_number in range(HEADS):
        first_col = head_number * head_width
        single_query_head = query_blocks[:, :, first_col:first_col + head_width]
        single_key_head = key_near[:, :, first_col:first_col + head_width]
        single_value_head = value_near[:, :, first_col:first_col + head_width]
        head_gradient = grad_blocks[:, :, first_col:first_col + head_width]
        attention_logits = LOGIT_SCALE * jnp.einsum('fdr,fwr->fdw', cast_to_single_float(single_query_head), cast_to_single_float(single_key_head))
        exponent = jnp.exp(attention_logits)
        attention_layer = exponent / lax.optimization_barrier(jnp.sum(exponent, axis=2, keepdims=True))
        weights_brain_float = cast_to_brain_float(attention_layer)
        attention_gradient = jnp.einsum('fdr,fwr->fdw', cast_to_single_float(head_gradient), cast_to_single_float(single_value_head))
        row_delta = lax.optimization_barrier(jnp.sum(attention_layer * attention_gradient, axis=2, keepdims=True))
        logit_gradient = cast_to_brain_float(LOGIT_SCALE * attention_layer * (attention_gradient - row_delta))
        query_pieces_list.append(jnp.einsum('xlj,xjr->xlr', cast_to_single_float(logit_gradient), cast_to_single_float(single_key_head)))
        neighbor_key_gradient = jnp.einsum('tsa,tsg->tag', cast_to_single_float(logit_gradient), cast_to_single_float(single_query_head)).reshape(block_list * neighbor_count, block_length, head_width)
        neighbor_value_gradient = jnp.einsum('tsa,tsg->tag', cast_to_single_float(weights_brain_float), cast_to_single_float(head_gradient)).reshape(block_list * neighbor_count, block_length, head_width)
        key_parts.append(jnp.einsum('ob,ote->bte', onehot, neighbor_key_gradient, precision=lax.Precision.HIGHEST))
        value_parts.append(jnp.einsum('ob,ote->bte', onehot, neighbor_value_gradient, precision=lax.Precision.HIGHEST))
    shape = query_rows.shape
    return (join_heads(query_pieces_list, shape), join_heads(key_parts, shape), join_heads(value_parts, shape))

def forward_channels(stream_rows, weights, neighbors):
    stream_float = cast_to_single_float(stream_rows)
    normed = cast_to_brain_float(row_norm(stream_float))
    raw_query, raw_key, query_rows, key_rows, value_rows = project(normed, weights)
    mixed_rows = attend_channels(query_rows, key_rows, value_rows, neighbors)
    output_rows = cast_to_brain_float(stream_float + jnp.dot(mixed_rows, weights[3], preferred_element_type=jnp.float32))
    return (output_rows, normed, raw_query, raw_key, value_rows, mixed_rows)

def backward_channels(stream_rows, normed, raw_query, raw_key, value_rows, mixed_rows, upstream_rows, weights, neighbors):
    out_grad = jnp.dot(mixed_rows.T, upstream_rows, preferred_element_type=jnp.float32)
    mixed_grad = cast_to_brain_float(jnp.dot(upstream_rows, weights[3].T, preferred_element_type=jnp.float32))
    query_rows = cast_to_brain_float(head_norm(raw_query))
    key_rows = cast_to_brain_float(head_norm(raw_key))
    query_grad, key_grad, value_grad = revert_channels(query_rows, key_rows, value_rows, neighbors, mixed_grad)
    normed_grad, weight_grads = project_back(normed, raw_query, raw_key, query_grad, key_grad, value_grad, weights)
    norm_back = jax.vjp(row_norm, cast_to_single_float(stream_rows))[1]
    stream_grad = cast_to_brain_float(cast_to_single_float(upstream_rows) + norm_back(normed_grad)[0])
    return (stream_grad, jnp.stack(weight_grads + [out_grad]))

def reference(series, upstream_grad, time_weights, channel_weights, neighbors):

    def sample_pass(sample_pair):
        series_rows, upstream_rows = sample_pair
        stream, stored = forward_time(series_rows, time_weights)

        def segment_pass(segment_pair):
            stream_seg, upstream_seg = segment_pair
            output_rows, normed, raw_query, raw_key, value_rows, mixed_rows = forward_channels(stream_seg, channel_weights, neighbors)
            stream_grad, grad_stack = backward_channels(stream_seg, normed, raw_query, raw_key, value_rows, mixed_rows, upstream_seg, channel_weights, neighbors)
            return (output_rows, stream_grad, grad_stack)
        outputs, stream_grads, channel_parts = lax.map(segment_pass, (jnp.swapaxes(stream, 0, 1), jnp.swapaxes(upstream_rows, 0, 1)))
        series_grad, time_part = backward_time(series_rows, stored, jnp.swapaxes(stream_grads, 0, 1), time_weights)
        return (jnp.swapaxes(outputs, 0, 1), series_grad, time_part, lax.optimization_barrier(jnp.sum(channel_parts, axis=0)))
    mixed_series, series_grad, time_parts, channel_parts = lax.map(sample_pass, (series, upstream_grad))
    time_grads = lax.optimization_barrier(jnp.sum(time_parts, axis=0)) / B
    channel_grads = lax.optimization_barrier(jnp.sum(channel_parts, axis=0)) / B
    return (mixed_series, series_grad, time_grads, channel_grads)
```

```python
import functools

import jax
import jax.numpy as jnp
from jax import lax
from jax.experimental import pallas as pl
from jax.experimental.pallas import tpu as pltpu
from jax.sharding import PartitionSpec as P

HEADS = 4
EPS = 1e-06
LOGIT_SCALE = 0.25
EXP2_SCALE = LOGIT_SCALE * 1.4426950408889634
GROUP = 128
TIME_ROWS = 512
PERM_ROWS = 256

F32 = jnp.float32
BF16 = jnp.bfloat16
MESH = pl.DeviceIdType.MESH


def mm(a, b):
    return lax.dot_general(a, b, (((1,), (0,)), ((), ())), preferred_element_type=F32)


def mm_nt(a, b):
    return lax.dot_general(a, b, (((1,), (1,)), ((), ())), preferred_element_type=F32)


def iota(shape, dim):
    return lax.broadcasted_iota(jnp.int32, shape, dim)


def eye(size):
    return jnp.where(iota((size, size), 0) == iota((size, size), 1), 1.0, 0.0).astype(BF16)


def regroup(outer, inner):
    size = outer * inner
    row, col = iota((size, size), 0), iota((size, size), 1)
    source = lax.rem(row, outer) * inner + row // outer
    return jnp.where(col == source, 1.0, 0.0).astype(BF16)


def head_blocks(features):
    width = features // HEADS
    rows = iota((features, features), 0) // width
    cols = iota((features, features), 1) // width
    return jnp.where(rows == cols, 1.0 / width, 0.0).astype(BF16)


def inv_rms(values):
    return lax.rsqrt(jnp.mean(values * values, axis=-1, keepdims=True) + EPS)


def head_hat(raw, blocks):
    inv = lax.rsqrt(mm((raw * raw).astype(BF16), blocks) + EPS)
    return (raw * inv).astype(BF16), inv


def head_back(hat_b, inv, grad, blocks):
    hat = hat_b.astype(F32)
    return (inv * (grad - hat * mm((hat * grad).astype(BF16), blocks))).astype(BF16)


def row_back(rows, grad):
    inv = inv_rms(rows)
    hat = rows * inv
    return inv * (grad - hat * jnp.mean(hat * grad, axis=-1, keepdims=True))


def fill_heads(ref, rows):
    width = rows.shape[1] // HEADS
    per_tile = GROUP // width
    tile_head = iota((GROUP, GROUP), 1) // width
    for h in range(HEADS):
        lanes = slice((h // per_tile) * GROUP, (h // per_tile + 1) * GROUP)
        keep = jnp.where(tile_head == h % per_tile, 1.0, 0.0).astype(BF16)
        ref[h * GROUP : (h + 1) * GROUP, lanes] = rows[:, lanes] * keep


def head_product(features_by_keys, keys_by_queries):
    features = features_by_keys.shape[0]
    width = features // HEADS
    per_tile = GROUP // width
    parts = []
    for tile in range(features // GROUP):
        cols = slice(tile * per_tile * GROUP, (tile + 1) * per_tile * GROUP)
        both = mm(features_by_keys[tile * GROUP : (tile + 1) * GROUP, :], keys_by_queries[:, cols])
        for h in range(per_tile):
            parts.append(both[h * width : (h + 1) * width, h * GROUP : (h + 1) * GROUP])
    return jnp.concatenate(parts, axis=0)


def others(axis, size):
    me = lax.axis_index(axis)
    return [lax.rem(me + k, size) for k in range(1, size)]


def aligned(start, size):
    return pl.ds(pl.multiple_of(start, size), size)


def layer_kernel(
    parts, dp, length,
    nb_ref, x_hbm, up_hbm, tw_ref, cw_ref,
    out_hbm, sgrad_hbm, tg_ref, cg_ref,
    x_s, up_raw, up_s, stream_s, cols_s, sg_s, ret_s,
    t_nT, t_q, t_k, t_kT, t_v, t_iq, t_ik, t_w, t_mT, t_sg, back_s,
    c_q, c_k, c_v, c_g, c_kT, c_vT, c_iq, c_ik, c_dq, c_dk, c_dv, c_m, c_mT, c_nT,
    qbd, gbd, tile_keep, acc_s, all_s, dp_in, mp_mine, mp_in, done_s, done_in,
    x_sem, up_sem, out_sem, grad_sem, in_send, in_recv, back_send, back_recv, last_send, last_recv,
    send1, recv1, send2, recv2, send3, recv3,
):
    segments, channels, features = up_s.shape
    own = stream_s.shape[1]
    rows_total = x_s.shape[0]
    chunks = rows_total // TIME_ROWS
    per_chunk = TIME_ROWS // length
    groups = TIME_ROWS // GROUP
    blocks_n, near = nb_ref.shape
    block = channels // blocks_n
    slots = qbd.shape[0]
    me = lax.axis_index("mp")
    me_dp = lax.axis_index("dp")
    peers = others("mp", parts)
    dp_peers = others("dp", dp)

    def load_x(t):
        return pltpu.make_async_copy(
            x_hbm.at[aligned(t * TIME_ROWS, TIME_ROWS)], x_s.at[aligned(t * TIME_ROWS, TIME_ROWS)], x_sem.at[t]
        )

    def load_up():
        return pltpu.make_async_copy(up_hbm, up_raw, up_sem)

    for t in range(chunks):
        load_x(t).start()
    load_up().start()

    barrier = pltpu.get_barrier_semaphore()
    for peer in peers:
        pl.semaphore_signal(barrier, inc=1, device_id={"mp": peer}, device_id_type=MESH)
    for peer in dp_peers:
        pl.semaphore_signal(barrier, inc=1, device_id={"dp": peer}, device_id_type=MESH)

    blocks = head_blocks(features)
    eye_f = eye(features)
    eye_g = eye(GROUP)
    cg = PERM_ROWS // length
    perm_t = regroup(cg, length)
    perm_tb = regroup(length, cg)
    sg_group = PERM_ROWS // segments
    qbd[...] = jnp.zeros_like(qbd)
    gbd[...] = jnp.zeros_like(gbd)
    tile_keep[...] = jnp.where(
        iota((GROUP, GROUP), 0) // length == iota((GROUP, GROUP), 1) // length, 1.0, 0.0
    ).astype(F32)
    c_dk[blocks_n * near] = jnp.zeros((block, features), F32)
    c_dv[blocks_n * near] = jnp.zeros((block, features), F32)
    pl.semaphore_wait(barrier, len(peers) + len(dp_peers))

    def inward(k, seg):
        return pltpu.make_async_remote_copy(
            src_ref=stream_s.at[peers[k] * segments + seg],
            dst_ref=cols_s.at[seg, aligned(me * own, own)],
            send_sem=in_send.at[k, seg],
            recv_sem=in_recv.at[k, seg],
            device_id={"mp": peers[k]},
            device_id_type=MESH,
        )

    def inward_part(k, t):
        return pltpu.make_async_remote_copy(
            src_ref=stream_s.at[peers[k] * segments, aligned(t * per_chunk, per_chunk)],
            dst_ref=cols_s.at[0, aligned(me * own + t * per_chunk, per_chunk)],
            send_sem=in_send.at[k, 0],
            recv_sem=in_recv.at[k, 0],
            device_id={"mp": peers[k]},
            device_id_type=MESH,
        )

    def back(k, seg):
        return pltpu.make_async_remote_copy(
            src_ref=sg_s.at[seg, aligned(peers[k] * own, own)],
            dst_ref=ret_s.at[me * segments + seg],
            send_sem=back_send.at[k, seg],
            recv_sem=back_recv.at[k, seg],
            device_id={"mp": peers[k]},
            device_id_type=MESH,
        )

    last = segments - 1

    def back_part(k, t):
        return pltpu.make_async_remote_copy(
            src_ref=sg_s.at[last, aligned(peers[k] * own + t * per_chunk, per_chunk)],
            dst_ref=ret_s.at[me * segments + last, aligned(t * per_chunk, per_chunk)],
            send_sem=last_send.at[k, t],
            recv_sem=last_recv.at[k, t],
            device_id={"mp": peers[k]},
            device_id_type=MESH,
        )

    def time_forward(t, carry):
        load_x(t).wait()
        rows = aligned(t * TIME_ROWS, TIME_ROWS)
        x = x_s[rows, :].astype(F32)
        normed = (x * inv_rms(x)).astype(BF16)
        t_nT[t] = mm_nt(eye_f, normed).astype(BF16)
        q, iq = head_hat(mm(normed, tw_ref[0]), blocks)
        k, ik = head_hat(mm(normed, tw_ref[1]), blocks)
        v = mm(normed, tw_ref[2]).astype(BF16)
        t_q[rows, :], t_k[rows, :], t_v[rows, :] = q, k, v
        t_iq[rows, :], t_ik[rows, :] = iq, ik
        t_kT[t] = mm_nt(eye_f, k).astype(BF16)
        vT = mm_nt(eye_f, v).astype(BF16)
        keep = jnp.concatenate([tile_keep[...]] * HEADS, axis=1)
        mixed = []
        for g in range(groups):
            sl = slice(g * GROUP, (g + 1) * GROUP)
            bd = qbd.at[g % slots]
            fill_heads(bd, q[sl])
            e = jnp.exp2(EXP2_SCALE * mm_nt(k[sl], bd[...])) * keep
            w = (e * (1.0 / jnp.sum(e, axis=0, keepdims=True))).astype(BF16)
            t_w[t * groups + g] = w
            mT = head_product(vT[:, sl], w).astype(BF16)
            t_mT[t, :, sl] = mT
            mixed.append(mm_nt(eye_g, mT).astype(BF16))
        stream = (x + mm(jnp.concatenate(mixed, axis=0), tw_ref[3])).astype(BF16)
        for part in range(TIME_ROWS // PERM_ROWS):
            ordered = mm(perm_t, stream[part * PERM_ROWS : (part + 1) * PERM_ROWS]).astype(BF16)
            for seg in range(length):
                stream_s[seg, aligned(t * per_chunk + part * cg, cg), :] = ordered[seg * cg : (seg + 1) * cg]
        for k_ in range(parts - 1):
            inward_part(k_, t).start()
        return carry

    lax.fori_loop(0, chunks, time_forward, 0)
    for seg in range(1, segments):
        for k in range(parts - 1):
            inward(k, seg).start()
    for seg in range(segments):
        cols_s[seg, aligned(me * own, own), :] = stream_s[me * segments + seg]

    load_up().wait()
    perm_u = regroup(sg_group, segments)
    perm_ub = regroup(segments, sg_group)
    for part in range(channels * segments // PERM_ROWS):
        ordered = mm(perm_u, up_raw[part * PERM_ROWS : (part + 1) * PERM_ROWS]).astype(BF16)
        for seg in range(segments):
            up_s[seg, part * sg_group : (part + 1) * sg_group, :] = ordered[seg * sg_group : (seg + 1) * sg_group]

    row_step = min(channels, 512)
    step_blocks = row_step // block

    def one_segment(seg, carry):
        for k in range(parts - 1):
            inward(k, seg).wait_recv()

        def project(r, inner):
            rows = aligned(r * row_step, row_step)
            these = pl.ds(r * step_blocks, step_blocks)
            x = cols_s[seg, rows, :].astype(F32)
            normed = (x * inv_rms(x)).astype(BF16)
            c_nT[seg, r] = mm_nt(eye_f, normed).astype(BF16)
            q, iq = head_hat(mm(normed, cw_ref[0]), blocks)
            k, ik = head_hat(mm(normed, cw_ref[1]), blocks)
            v = mm(normed, cw_ref[2]).astype(BF16)
            shaped = (step_blocks, block, features)
            c_q[these], c_k[these], c_v[these] = q.reshape(shaped), k.reshape(shaped), v.reshape(shaped)
            c_iq[these], c_ik[these] = iq.reshape(shaped), ik.reshape(shaped)
            kT = mm_nt(eye_f, k).astype(BF16)
            vT = mm_nt(eye_f, v).astype(BF16)
            for b in range(step_blocks):
                c_kT[r * step_blocks + b] = kT[:, b * block : (b + 1) * block]
                c_vT[r * step_blocks + b] = vT[:, b * block : (b + 1) * block]
            c_g[these] = mm_nt(up_s[seg, rows, :], cw_ref[3]).astype(BF16).reshape(shaped)
            return inner

        lax.fori_loop(0, channels // row_step, project, 0)

        def attend(pair, inner):
            for slot in range(slots):
                i = pair * slots + slot
                ids = [nb_ref[i, n] for n in range(near)]
                bd, gd = qbd.at[slot], gbd.at[slot]
                fill_heads(bd, c_q[i])
                fill_heads(gd, c_g[i])
                k_near = jnp.concatenate([c_k[j] for j in ids], axis=0)
                v_near = jnp.concatenate([c_v[j] for j in ids], axis=0)
                kT_near = jnp.concatenate([c_kT[j] for j in ids], axis=1)
                vT_near = jnp.concatenate([c_vT[j] for j in ids], axis=1)
                e = jnp.exp2(EXP2_SCALE * mm_nt(k_near, bd[...]))
                w = e * (1.0 / jnp.sum(e, axis=0, keepdims=True))
                w_b = w.astype(BF16)
                grad = mm_nt(v_near, gd[...])
                delta = jnp.sum(w * grad, axis=0, keepdims=True)
                t_b = (w * (grad - delta)).astype(BF16)
                mT = head_product(vT_near, w_b).astype(BF16)
                c_mT[seg, i] = mT
                c_m[seg, aligned(i * block, block), :] = mm_nt(eye_g, mT).astype(BF16)
                dqT = (LOGIT_SCALE * head_product(kT_near, t_b)).astype(BF16)
                c_dq[i] = mm_nt(eye_g, dqT).astype(BF16)
                c_dk[pl.ds(i * near, near)] = mm(t_b, bd[...]).reshape(near, block, features)
                c_dv[pl.ds(i * near, near)] = mm(w_b, gd[...]).reshape(near, block, features)
            return inner

        lax.fori_loop(0, blocks_n // slots, attend, 0)

        def finish(j, inner):
            def place(i):
                at = blocks_n * near
                for n in range(1, near):
                    at = jnp.where(nb_ref[i, n] == j, i * near + n, at)
                return at

            def more(m, sums):
                at = place(lax.rem(j + m, blocks_n))
                return sums[0] + c_dk[at], sums[1] + c_dv[at]

            sums = (c_dk[j * near], c_dv[j * near])
            if blocks_n <= 4:
                for m in range(1, blocks_n):
                    sums = more(m, sums)
            else:
                sums = lax.fori_loop(1, blocks_n, more, sums)
            rows = aligned(j * block, block)
            qb = head_back(c_q[j], c_iq[j], c_dq[j].astype(F32), blocks)
            kb = head_back(c_k[j], c_ik[j], LOGIT_SCALE * sums[0], blocks)
            vb = sums[1].astype(BF16)
            at_rows = aligned(seg * channels + j * block, block)
            back_s[0, at_rows, :] = qb
            back_s[1, at_rows, :] = kb
            back_s[2, at_rows, :] = vb
            grad = mm_nt(qb, cw_ref[0]) + mm_nt(kb, cw_ref[1]) + mm_nt(vb, cw_ref[2])
            x = cols_s[seg, rows, :].astype(F32)
            sg_s[seg, rows, :] = (up_s[seg, rows, :].astype(F32) + row_back(x, grad)).astype(BF16)
            return inner

        lax.fori_loop(0, blocks_n, finish, 0)

        @pl.when(seg < last)
        def _():
            for k in range(parts - 1):
                back(k, seg).start()

        ret_s[me * segments + seg] = sg_s[seg, aligned(me * own, own), :]
        return carry

    lax.fori_loop(0, segments, one_segment, 0)
    for t in range(chunks):
        for k in range(parts - 1):
            back_part(k, t).start()

    matrices = tw_ref.shape[0]
    width = all_s.shape[3]
    splits = features // width

    def exchange(src, dst, send, recv, device):
        return pltpu.make_async_remote_copy(
            src_ref=src, dst_ref=dst, send_sem=send, recv_sem=recv, device_id=device, device_id_type=MESH
        )

    def put_grad(r, m, value):
        for part in range(splits):
            all_s[r, m * splits + part] = value[:, part * width : (part + 1) * width].astype(BF16)

    def stage1(r):
        return [
            exchange(all_s.at[r, p], dp_in.at[r, k], send1.at[r, k], recv1.at[r, k], {"dp": p})
            for k, p in enumerate(dp_peers)
        ]

    def stage2(r):
        return [
            exchange(mp_mine.at[r, p], mp_in.at[r, k], send2.at[r, k], recv2.at[r, k], {"mp": p})
            for k, p in enumerate(peers)
        ]

    def stage3(r):
        return [
            exchange(done_s.at[r], done_in.at[r, me_dp], send3.at[r, k], recv3.at[r, k], {"dp": p})
            for k, p in enumerate(dp_peers)
        ]

    def start(copies):
        for copy in copies:
            copy.start()

    def wait(copies):
        for copy in copies:
            copy.wait()

    def finish1(r):
        wait(stage1(r))
        total = all_s[r, me_dp].astype(F32)
        for k in range(dp - 1):
            total = total + dp_in[r, k].astype(F32)
        mp_mine[r] = total.astype(BF16).reshape(mp_mine.shape[1:])
        start(stage2(r))

    def finish2(r):
        wait(stage2(r))
        total = mp_mine[r, me].astype(F32)
        for k in range(parts - 1):
            total = total + mp_in[r, k].astype(F32)
        done_s[r] = total.astype(BF16)
        start(stage3(r))
        done_in[r, me_dp] = done_s[r]

    def finish3(r, ref):
        wait(stage3(r))
        for m in range(matrices):
            for part in range(splits):
                ref[m, :, part * width : (part + 1) * width] = done_in[r, m * splits + part].astype(F32) / dp

    steps = channels // row_step
    for m in range(matrices):
        total = None
        for seg in range(segments):
            for r in range(steps):
                rows = slice(r * row_step, (r + 1) * row_step)
                if m < 3:
                    term = mm(c_nT[seg, r], back_s[m, seg * channels + r * row_step : seg * channels + (r + 1) * row_step, :])
                else:
                    mT = jnp.concatenate([c_mT[seg, r * step_blocks + b] for b in range(step_blocks)], axis=1)
                    term = mm(mT, up_s[seg, rows, :])
                total = term if total is None else total + term
        put_grad(1, m, total)
    start(stage1(1))

    for seg in range(segments):
        for r in range(steps):
            rows = slice(r * row_step, (r + 1) * row_step)
            res = cols_s[seg, rows, :].astype(F32) + mm(c_m[seg, rows, :], cw_ref[3])
            c_m[seg, rows, :] = res.astype(BF16)
    for part in range(channels * segments // PERM_ROWS):
        lanes = slice(part * sg_group, (part + 1) * sg_group)
        mixed = jnp.concatenate([c_m[seg, lanes, :] for seg in range(segments)], axis=0)
        up_raw[part * PERM_ROWS : (part + 1) * PERM_ROWS, :] = mm(perm_ub, mixed).astype(BF16)
    out_copy = pltpu.make_async_copy(up_raw, out_hbm, out_sem)
    out_copy.start()

    for seg in range(last):
        for k in range(parts - 1):
            back(k, seg).wait_recv()

    def time_backward(t, carry):
        for k in range(parts - 1):
            back_part(k, t).wait_recv()
        rows = aligned(t * TIME_ROWS, TIME_ROWS)
        ordered = []
        for part in range(TIME_ROWS // PERM_ROWS):
            at = aligned(t * per_chunk + part * cg, cg)
            slabs = jnp.concatenate([ret_s[seg, at, :] for seg in range(length)], axis=0)
            ordered.append(mm(perm_tb, slabs).astype(BF16))
        up_b = jnp.concatenate(ordered, axis=0)
        t_sg[rows, :] = up_b
        mg = mm_nt(up_b, tw_ref[3]).astype(BF16)
        q, k, v = t_q[rows, :], t_k[rows, :], t_v[rows, :]
        kT = t_kT[t]
        dq, dk, dv = [], [], []
        for g in range(groups):
            sl = slice(g * GROUP, (g + 1) * GROUP)
            bd, gd = qbd.at[g % slots], gbd.at[g % slots]
            fill_heads(bd, q[sl])
            fill_heads(gd, mg[sl])
            w_b = t_w[t * groups + g]
            w = w_b.astype(F32)
            grad = mm_nt(v[sl], gd[...])
            delta = jnp.sum(w * grad, axis=0, keepdims=True)
            t_b = (w * (grad - delta)).astype(BF16)
            dqT = (LOGIT_SCALE * head_product(kT[:, sl], t_b)).astype(BF16)
            dq.append(mm_nt(eye_g, dqT))
            dk.append(LOGIT_SCALE * mm(t_b, bd[...]))
            dv.append(mm(w_b, gd[...]).astype(BF16))
        qb = head_back(q, t_iq[rows, :], jnp.concatenate(dq, axis=0), blocks)
        kb = head_back(k, t_ik[rows, :], jnp.concatenate(dk, axis=0), blocks)
        vb = jnp.concatenate(dv, axis=0)
        back_s[0, rows, :] = qb
        back_s[1, rows, :] = kb
        back_s[2, rows, :] = vb
        nT = t_nT[t]
        first = t == 0
        for m, back_rows in enumerate((qb, kb, vb)):
            acc_s[m] = mm(nT, back_rows) + jnp.where(first, 0.0, acc_s[m])
        acc_s[3] = mm(t_mT[t], up_b) + jnp.where(first, 0.0, acc_s[3])
        return carry

    acc_s[...] = jnp.zeros_like(acc_s)
    lax.fori_loop(0, 1, time_backward, 0)
    finish1(1)
    lax.fori_loop(1, 2, time_backward, 0)
    finish2(1)
    lax.fori_loop(2, 3, time_backward, 0)
    finish3(1, cg_ref)
    lax.fori_loop(3, chunks, time_backward, 0)
    for m in range(matrices):
        put_grad(0, m, acc_s[m])
    start(stage1(0))

    def series_back(t, carry):
        rows = aligned(t * TIME_ROWS, TIME_ROWS)
        grad = mm_nt(back_s[0, rows, :], tw_ref[0]) + mm_nt(back_s[1, rows, :], tw_ref[1])
        grad = grad + mm_nt(back_s[2, rows, :], tw_ref[2])
        x = x_s[rows, :].astype(F32)
        t_sg[rows, :] = (t_sg[rows, :].astype(F32) + row_back(x, grad)).astype(BF16)
        return carry

    lax.fori_loop(0, chunks, series_back, 0)
    grad_copy = pltpu.make_async_copy(t_sg, sgrad_hbm, grad_sem)
    grad_copy.start()
    finish1(0)
    finish2(0)
    finish3(0, tg_ref)

    grad_copy.wait()
    out_copy.wait()
    for k in range(parts - 1):
        for seg in range(segments):
            inward(k, seg).wait_send()
        for seg in range(last):
            back(k, seg).wait_send()
        for t in range(chunks):
            back_part(k, t).wait_send()


VMEM_LIMIT = 62 * 1024 * 1024


def shards(series, upstream_grad, time_weights, channel_weights, neighbors):
    parts, dp = lax.axis_size("mp"), lax.axis_size("dp")
    own, length, features = series.shape[1:]
    channels, segments = upstream_grad.shape[1:3]
    blocks_n, near = neighbors.shape
    block = channels // blocks_n
    matrices = time_weights.shape[0]
    total = own * length
    chunks = total // TIME_ROWS
    row_step = min(channels, 512)
    steps = channels // row_step
    slots = 2
    mine = features // parts
    width = features * matrices // dp
    vmem = pl.BlockSpec(memory_space=pltpu.VMEM)
    hbm = pl.BlockSpec(memory_space=pl.ANY)
    dma = lambda *shape: pltpu.SemaphoreType.DMA(shape)
    b16 = lambda *shape: pltpu.VMEM(shape, BF16)
    f32 = lambda *shape: pltpu.VMEM(shape, F32)
    grads = jax.ShapeDtypeStruct((matrices, mine, features), F32)
    per_block = (blocks_n, block, features)
    contributions = f32(blocks_n * near + 1, block, features)
    output, series_grad, time_grads, channel_grads = pl.pallas_call(
        functools.partial(layer_kernel, parts, dp, length),
        out_shape=(
            jax.ShapeDtypeStruct((channels * segments, features), BF16),
            jax.ShapeDtypeStruct((total, features), BF16),
            grads,
            grads,
        ),
        in_specs=[pl.BlockSpec(memory_space=pltpu.SMEM), hbm, hbm, vmem, vmem],
        out_specs=(hbm, hbm, vmem, vmem),
        scratch_shapes=[
            b16(total, features),
            b16(channels * segments, features),
            b16(segments, channels, features),
            b16(length, own, features),
            b16(segments, channels, features),
            b16(segments, channels, features),
            b16(length, own, features),
            b16(chunks, features, TIME_ROWS),
            b16(total, features),
            b16(total, features),
            b16(chunks, features, TIME_ROWS),
            b16(total, features),
            f32(total, features),
            f32(total, features),
            b16(total // GROUP, GROUP, HEADS * GROUP),
            b16(chunks, features, TIME_ROWS),
            b16(total, features),
            b16(3, total, features),
            b16(*per_block),
            b16(*per_block),
            b16(*per_block),
            b16(*per_block),
            b16(blocks_n, features, block),
            b16(blocks_n, features, block),
            f32(*per_block),
            f32(*per_block),
            b16(*per_block),
            contributions,
            contributions,
            b16(segments, channels, features),
            b16(segments, blocks_n, features, block),
            b16(segments, steps, features, row_step),
            b16(slots, HEADS * GROUP, features),
            b16(slots, HEADS * GROUP, features),
            f32(GROUP, GROUP),
            f32(matrices, features, features),
            b16(2, dp, features, width),
            b16(2, dp - 1, features, width),
            b16(2, parts, mine, width),
            b16(2, parts - 1, mine, width),
            b16(2, mine, width),
            b16(2, dp, mine, width),
            dma(chunks), pltpu.SemaphoreType.DMA, pltpu.SemaphoreType.DMA, pltpu.SemaphoreType.DMA,
            dma(parts - 1, segments), dma(parts - 1, segments),
            dma(parts - 1, segments), dma(parts - 1, segments),
            dma(parts - 1, chunks), dma(parts - 1, chunks),
            dma(2, dp - 1), dma(2, dp - 1), dma(2, parts - 1), dma(2, parts - 1), dma(2, dp - 1), dma(2, dp - 1),
        ],
        compiler_params=pltpu.CompilerParams(
            vmem_limit_bytes=VMEM_LIMIT, collective_id=0, has_side_effects=True
        ),
        name="layer",
    )(
        neighbors,
        series.reshape(total, features),
        upstream_grad.reshape(channels * segments, features),
        time_weights,
        channel_weights,
    )
    return (
        output.reshape(upstream_grad.shape),
        series_grad.reshape(series.shape),
        time_grads,
        channel_grads,
    )


def solution(mesh):
    placed = (P("dp", "mp", None, None), P("dp", None, "mp", None), P(), P(), P())
    return jax.shard_map(
        shards,
        mesh=mesh,
        in_specs=placed,
        out_specs=(
            P("dp", None, "mp", None),
            P("dp", "mp", None, None),
            P(None, "mp", None),
            P(None, "mp", None),
        ),
        check_vma=False,
    )
```

```python
import functools

import jax
import jax.numpy as jnp
from jax import lax
from jax.experimental import pallas as pl
from jax.experimental.pallas import tpu as pltpu
from jax.sharding import PartitionSpec as P

HEADS = 4
EPS = 1e-06
LOGIT_SCALE = 0.25
EXP2_SCALE = LOGIT_SCALE * 1.4426950408889634
GROUP = 128
TIME_ROWS = 512
PERM_ROWS = 256

F32 = jnp.float32
BF16 = jnp.bfloat16
MESH = pl.DeviceIdType.MESH


def mm(a, b):
    return lax.dot_general(a, b, (((1,), (0,)), ((), ())), preferred_element_type=F32)


def mm_nt(a, b):
    return lax.dot_general(a, b, (((1,), (1,)), ((), ())), preferred_element_type=F32)


def iota(shape, dim):
    return lax.broadcasted_iota(jnp.int32, shape, dim)


def eye(size):
    return jnp.where(iota((size, size), 0) == iota((size, size), 1), 1.0, 0.0).astype(BF16)


def regroup(outer, inner):
    size = outer * inner
    row, col = iota((size, size), 0), iota((size, size), 1)
    source = lax.rem(row, outer) * inner + row // outer
    return jnp.where(col == source, 1.0, 0.0).astype(BF16)


def head_blocks(features):
    width = features // HEADS
    rows = iota((features, features), 0) // width
    cols = iota((features, features), 1) // width
    return jnp.where(rows == cols, 1.0 / width, 0.0).astype(BF16)


def inv_rms(values):
    return lax.rsqrt(jnp.mean(values * values, axis=-1, keepdims=True) + EPS)


def head_hat(raw, blocks):
    inv = lax.rsqrt(mm((raw * raw).astype(BF16), blocks) + EPS)
    return (raw * inv).astype(BF16), inv


def head_back(hat_b, inv, grad, blocks):
    hat = hat_b.astype(F32)
    return (inv * (grad - hat * mm((hat * grad).astype(BF16), blocks))).astype(BF16)


def row_back(rows, grad):
    inv = inv_rms(rows)
    hat = rows * inv
    return inv * (grad - hat * jnp.mean(hat * grad, axis=-1, keepdims=True))


def fill_heads(ref, rows):
    width = rows.shape[1] // HEADS
    per_tile = GROUP // width
    tile_head = iota((GROUP, GROUP), 1) // width
    for h in range(HEADS):
        lanes = slice((h // per_tile) * GROUP, (h // per_tile + 1) * GROUP)
        keep = jnp.where(tile_head == h % per_tile, 1.0, 0.0).astype(BF16)
        ref[h * GROUP : (h + 1) * GROUP, lanes] = rows[:, lanes] * keep


def head_product(features_by_keys, keys_by_queries):
    features = features_by_keys.shape[0]
    width = features // HEADS
    per_tile = GROUP // width
    parts = []
    for tile in range(features // GROUP):
        cols = slice(tile * per_tile * GROUP, (tile + 1) * per_tile * GROUP)
        both = mm(features_by_keys[tile * GROUP : (tile + 1) * GROUP, :], keys_by_queries[:, cols])
        for h in range(per_tile):
            parts.append(both[h * width : (h + 1) * width, h * GROUP : (h + 1) * GROUP])
    return jnp.concatenate(parts, axis=0)


def others(axis, size):
    me = lax.axis_index(axis)
    return [lax.rem(me + k, size) for k in range(1, size)]


def aligned(start, size):
    return pl.ds(pl.multiple_of(start, size), size)


def layer_kernel(
    parts, dp, length,
    nb_ref, x_hbm, up_hbm, tw_ref, cw_ref,
    out_hbm, sgrad_hbm, tg_ref, cg_ref,
    x_s, up_raw, up_s, stream_s, cols_s, sg_s, ret_s,
    t_nT, t_q, t_k, t_kT, t_v, t_iq, t_ik, t_w, t_mT, t_sg, back_s,
    c_q, c_k, c_v, c_g, c_kT, c_vT, c_iq, c_ik, c_dq, c_dk, c_dv, c_m, c_mT, c_nT,
    qbd, gbd, tile_keep, acc_s, all_s, core_in, chip_s, dp_in, mp_mine, mp_in, done_s, done_in,
    x_sem, up_sem, out_sem, grad_sem, in_send, in_recv, back_send, back_recv, last_send, last_recv,
    send0, recv0, send1, recv1, send2, recv2, send3, recv3,
):
    segments, channels, features = up_s.shape
    own = stream_s.shape[1]
    rows_total = x_s.shape[0]
    chunks = rows_total // TIME_ROWS
    per_chunk = TIME_ROWS // length
    groups = TIME_ROWS // GROUP
    blocks_n, near = nb_ref.shape
    block = channels // blocks_n
    slots = qbd.shape[0]
    me = lax.axis_index("mp")
    me_dp = lax.axis_index("dp")
    peers = others("mp", parts)
    dp_peers = others("dp", dp)

    def load_x(t):
        return pltpu.make_async_copy(
            x_hbm.at[aligned(t * TIME_ROWS, TIME_ROWS)], x_s.at[aligned(t * TIME_ROWS, TIME_ROWS)], x_sem.at[t]
        )

    def load_up():
        return pltpu.make_async_copy(up_hbm, up_raw, up_sem)

    for t in range(chunks):
        load_x(t).start()
    load_up().start()

    barrier = pltpu.get_barrier_semaphore()
    for peer in peers:
        pl.semaphore_signal(barrier, inc=1, device_id={"mp": peer}, device_id_type=MESH)
    for peer in dp_peers:
        pl.semaphore_signal(barrier, inc=1, device_id={"dp": peer}, device_id_type=MESH)

    blocks = head_blocks(features)
    cg = PERM_ROWS // length
    perm_t = regroup(cg, length)
    perm_tb = regroup(length, cg)
    tiles = features // GROUP
    sg_group = PERM_ROWS // (tiles * segments)
    qbd[...] = jnp.zeros_like(qbd)
    gbd[...] = jnp.zeros_like(gbd)
    tile_keep[...] = jnp.where(
        iota((GROUP, GROUP), 0) // length == iota((GROUP, GROUP), 1) // length, 1.0, 0.0
    ).astype(F32)
    c_dk[blocks_n * near] = jnp.zeros((block, features), F32)
    c_dv[blocks_n * near] = jnp.zeros((block, features), F32)

    def inward(k, seg):
        return pltpu.make_async_remote_copy(
            src_ref=stream_s.at[peers[k] * segments + seg],
            dst_ref=cols_s.at[seg, aligned(me * own, own)],
            send_sem=in_send.at[k, seg],
            recv_sem=in_recv.at[k, seg],
            device_id={"mp": peers[k]},
            device_id_type=MESH,
        )

    def inward_part(k, seg, t):
        return pltpu.make_async_remote_copy(
            src_ref=stream_s.at[peers[k] * segments + seg, aligned(t * per_chunk, per_chunk)],
            dst_ref=cols_s.at[seg, aligned(me * own + t * per_chunk, per_chunk)],
            send_sem=in_send.at[k, seg],
            recv_sem=in_recv.at[k, seg],
            device_id={"mp": peers[k]},
            device_id_type=MESH,
        )

    def back(k, seg):
        return pltpu.make_async_remote_copy(
            src_ref=sg_s.at[seg, aligned(peers[k] * own, own)],
            dst_ref=ret_s.at[me * segments + seg],
            send_sem=back_send.at[k, seg],
            recv_sem=back_recv.at[k, seg],
            device_id={"mp": peers[k]},
            device_id_type=MESH,
        )

    last = segments - 1

    def back_part(k, t):
        return pltpu.make_async_remote_copy(
            src_ref=sg_s.at[last, aligned(peers[k] * own + t * per_chunk, per_chunk)],
            dst_ref=ret_s.at[me * segments + last, aligned(t * per_chunk, per_chunk)],
            send_sem=last_send.at[k, t],
            recv_sem=last_recv.at[k, t],
            device_id={"mp": peers[k]},
            device_id_type=MESH,
        )

    def time_forward(t, carry):
        load_x(t).wait()
        rows = aligned(t * TIME_ROWS, TIME_ROWS)
        x = x_s[rows, :].astype(F32)
        normed = (x * inv_rms(x)).astype(BF16)
        t_nT[t] = normed.T
        q, iq = head_hat(mm(normed, tw_ref[0]), blocks)
        k, ik = head_hat(mm(normed, tw_ref[1]), blocks)
        v = mm(normed, tw_ref[2]).astype(BF16)
        t_q[rows, :], t_k[rows, :], t_v[rows, :] = q, k, v
        t_iq[rows, :], t_ik[rows, :] = iq, ik
        t_kT[t] = k.T
        vT = v.T
        keep = jnp.concatenate([tile_keep[...]] * HEADS, axis=1)
        mixed = []
        for g in range(groups):
            sl = slice(g * GROUP, (g + 1) * GROUP)
            bd = qbd.at[g % slots]
            fill_heads(bd, q[sl])
            e = jnp.exp2(EXP2_SCALE * mm_nt(k[sl], bd[...])) * keep
            w = (e * (1.0 / jnp.sum(e, axis=0, keepdims=True))).astype(BF16)
            t_w[t * groups + g] = w
            mT = head_product(vT[:, sl], w).astype(BF16)
            t_mT[t, :, sl] = mT
            mixed.append(mT.T)
        stream = (x + mm(jnp.concatenate(mixed, axis=0), tw_ref[3])).astype(BF16)
        for part in range(TIME_ROWS // PERM_ROWS):
            ordered = mm(perm_t, stream[part * PERM_ROWS : (part + 1) * PERM_ROWS]).astype(BF16)
            for seg in range(length):
                stream_s[seg, aligned(t * per_chunk + part * cg, cg), :] = ordered[seg * cg : (seg + 1) * cg]
        @pl.when(t == 0)
        def _():
            pl.semaphore_wait(barrier, len(peers) + len(dp_peers))

        for peer in range(parts - 1):
            inward_part(peer, 0, t).start()
        if segments > 1:

            @pl.when(t < chunks // 2)
            def _():
                for peer in range(parts - 1):
                    inward_part(peer, 1, t).start()

        return carry

    lax.fori_loop(0, chunks, time_forward, 0)
    for seg in range(1, segments):
        for k in range(parts - 1):
            if seg == 1:
                for t in range(chunks // 2, chunks):
                    inward_part(k, seg, t).start()
            else:
                inward(k, seg).start()
    for seg in range(segments):
        cols_s[seg, aligned(me * own, own), :] = stream_s[me * segments + seg]

    load_up().wait()
    perm_u = regroup(sg_group, tiles * segments)
    perm_ub = regroup(tiles * segments, sg_group)

    def order_up(pair, carry):
        both = [up_raw[aligned((pair * 2 + n) * PERM_ROWS, PERM_ROWS), :] for n in range(2)]
        ordered = mm(perm_u, jnp.concatenate(both, axis=1)).astype(BF16)
        for n in range(2):
            for tile in range(tiles):
                for seg in range(segments):
                    at = (tile * segments + seg) * sg_group
                    up_s[seg, aligned((pair * 2 + n) * sg_group, sg_group), tile * GROUP : (tile + 1) * GROUP] = ordered[
                        at : at + sg_group, n * GROUP : (n + 1) * GROUP
                    ]
        return carry

    lax.fori_loop(0, channels // (2 * sg_group), order_up, 0, unroll=True)

    row_step = min(channels, 512)
    step_blocks = row_step // block

    def one_segment(seg, carry):
        for k in range(parts - 1):
            inward(k, seg).wait_recv()

        def project(r, inner):
            rows = aligned(r * row_step, row_step)
            these = pl.ds(r * step_blocks, step_blocks)
            x = cols_s[seg, rows, :].astype(F32)
            normed = (x * inv_rms(x)).astype(BF16)
            c_nT[seg, r] = normed.T
            q, iq = head_hat(mm(normed, cw_ref[0]), blocks)
            k, ik = head_hat(mm(normed, cw_ref[1]), blocks)
            v = mm(normed, cw_ref[2]).astype(BF16)
            shaped = (step_blocks, block, features)
            c_q[these], c_k[these], c_v[these] = q.reshape(shaped), k.reshape(shaped), v.reshape(shaped)
            c_iq[these], c_ik[these] = iq.reshape(shaped), ik.reshape(shaped)
            kT = k.T
            vT = v.T
            for b in range(step_blocks):
                c_kT[r * step_blocks + b] = kT[:, b * block : (b + 1) * block]
                c_vT[r * step_blocks + b] = vT[:, b * block : (b + 1) * block]
            c_g[these] = mm_nt(up_s[seg, rows, :], cw_ref[3]).astype(BF16).reshape(shaped)
            return inner

        lax.fori_loop(0, channels // row_step, project, 0)

        def attend(pair, inner):
            for slot in range(slots):
                i = pair * slots + slot
                ids = [nb_ref[i, n] for n in range(near)]
                bd, gd = qbd.at[slot], gbd.at[slot]
                fill_heads(bd, c_q[i])
                fill_heads(gd, c_g[i])
                k_near = jnp.concatenate([c_k[j] for j in ids], axis=0)
                v_near = jnp.concatenate([c_v[j] for j in ids], axis=0)
                kT_near = jnp.concatenate([c_kT[j] for j in ids], axis=1)
                vT_near = jnp.concatenate([c_vT[j] for j in ids], axis=1)
                e = jnp.exp2(EXP2_SCALE * mm_nt(k_near, bd[...]))
                w = e * (1.0 / jnp.sum(e, axis=0, keepdims=True))
                w_b = w.astype(BF16)
                grad = mm_nt(v_near, gd[...])
                delta = jnp.sum(w * grad, axis=0, keepdims=True)
                t_b = (w * (grad - delta)).astype(BF16)
                mT = head_product(vT_near, w_b).astype(BF16)
                c_mT[seg, i] = mT
                c_m[seg, aligned(i * block, block), :] = mT.T
                dqT = (LOGIT_SCALE * head_product(kT_near, t_b)).astype(BF16)
                c_dq[i] = dqT.T
                c_dk[pl.ds(i * near, near)] = mm(t_b, bd[...]).reshape(near, block, features)
                c_dv[pl.ds(i * near, near)] = mm(w_b, gd[...]).reshape(near, block, features)
            return inner

        lax.fori_loop(0, blocks_n // slots, attend, 0)

        def finish_block(j):
            def place(i):
                at = blocks_n * near
                for n in range(1, near):
                    at = jnp.where(nb_ref[i, n] == j, i * near + n, at)
                return at

            def more(m, sums):
                at = place(lax.rem(j + m, blocks_n))
                return sums[0] + c_dk[at], sums[1] + c_dv[at]

            sums = (c_dk[j * near], c_dv[j * near])
            if blocks_n <= 4:
                for m in range(1, blocks_n):
                    sums = more(m, sums)
            else:
                sums = lax.fori_loop(1, blocks_n, more, sums)
            rows = aligned(j * block, block)
            qb = head_back(c_q[j], c_iq[j], c_dq[j].astype(F32), blocks)
            kb = head_back(c_k[j], c_ik[j], LOGIT_SCALE * sums[0], blocks)
            vb = sums[1].astype(BF16)
            at_rows = aligned(seg * channels + j * block, block)
            back_s[0, at_rows, :] = qb
            back_s[1, at_rows, :] = kb
            back_s[2, at_rows, :] = vb
            grad = mm_nt(qb, cw_ref[0]) + mm_nt(kb, cw_ref[1]) + mm_nt(vb, cw_ref[2])
            x = cols_s[seg, rows, :].astype(F32)
            sg_s[seg, rows, :] = (up_s[seg, rows, :].astype(F32) + row_back(x, grad)).astype(BF16)

        def finish(group, inner):
            for n in range(slots):
                finish_block(group * slots + n)
            return inner

        lax.fori_loop(0, blocks_n // slots, finish, 0)

        @pl.when(seg < last)
        def _():
            for k in range(parts - 1):
                back(k, seg).start()

        ret_s[me * segments + seg] = sg_s[seg, aligned(me * own, own), :]
        return carry

    lax.fori_loop(0, segments, one_segment, 0)
    for t in range(chunks):
        for k in range(parts - 1):
            back_part(k, t).start()

    matrices = tw_ref.shape[0]
    width = all_s.shape[4]
    core, chip = lax.rem(me_dp, 2), me_dp // 2
    chips = dp // 2
    chip_peers = [lax.rem(chip + k, chips) for k in range(1, chips)]
    splits = features // width

    def exchange(src, dst, send, recv, device):
        return pltpu.make_async_remote_copy(
            src_ref=src, dst_ref=dst, send_sem=send, recv_sem=recv, device_id=device, device_id_type=MESH
        )

    def put_grad(r, m, value):
        for part in range(splits):
            place = m * splits + part
            all_s[r, place % 2, place // 2] = value[:, part * width : (part + 1) * width].astype(BF16)

    def stage0(r):
        return [exchange(all_s.at[r, 1 - core], core_in.at[r], send0.at[r], recv0.at[r], {"dp": me_dp + 1 - 2 * core})]

    def stage1(r):
        return [
            exchange(chip_s.at[r, p], dp_in.at[r, k], send1.at[r, k], recv1.at[r, k], {"dp": p * 2 + core})
            for k, p in enumerate(chip_peers)
        ]

    def stage2(r):
        return [
            exchange(mp_mine.at[r, p], mp_in.at[r, k], send2.at[r, k], recv2.at[r, k], {"mp": p})
            for k, p in enumerate(peers)
        ]

    def stage3(r):
        return [
            exchange(done_s.at[r], done_in.at[r, me_dp], send3.at[r, k], recv3.at[r, k], {"dp": p})
            for k, p in enumerate(dp_peers)
        ]

    def start(copies):
        for copy in copies:
            copy.start()

    def wait(copies):
        for copy in copies:
            copy.wait()

    def finish0(r):
        wait(stage0(r))
        chip_s[r] = (all_s[r, core].astype(F32) + core_in[r].astype(F32)).astype(BF16)
        start(stage1(r))

    def finish1(r):
        wait(stage1(r))
        total = chip_s[r, chip].astype(F32)
        for k in range(chips - 1):
            total = total + dp_in[r, k].astype(F32)
        mp_mine[r] = total.astype(BF16).reshape(mp_mine.shape[1:])
        start(stage2(r))

    def finish2(r):
        wait(stage2(r))
        total = mp_mine[r, me].astype(F32)
        for k in range(parts - 1):
            total = total + mp_in[r, k].astype(F32)
        done_s[r] = total.astype(BF16)
        start(stage3(r))
        done_in[r, me_dp] = done_s[r]

    def finish3(r, ref):
        wait(stage3(r))
        for m in range(matrices):
            for part in range(splits):
                ref[m, :, part * width : (part + 1) * width] = done_in[r, m * splits + part].astype(F32) / dp

    steps = channels // row_step
    for m in range(matrices):
        total = None
        for seg in range(segments):
            for r in range(steps):
                rows = slice(r * row_step, (r + 1) * row_step)
                if m < 3:
                    term = mm(c_nT[seg, r], back_s[m, seg * channels + r * row_step : seg * channels + (r + 1) * row_step, :])
                else:
                    mT = jnp.concatenate([c_mT[seg, r * step_blocks + b] for b in range(step_blocks)], axis=1)
                    term = mm(mT, up_s[seg, rows, :])
                total = term if total is None else total + term
        put_grad(1, m, total)
    start(stage0(1))


    def project_out(r, carry):
        rows = aligned(r * row_step, row_step)
        for seg in range(segments):
            res = cols_s[seg, rows, :].astype(F32) + mm(c_m[seg, rows, :], cw_ref[3])
            c_m[seg, rows, :] = res.astype(BF16)
        return carry

    def order_out(pair, carry):
        both = []
        for n in range(2):
            rows = aligned((pair * 2 + n) * sg_group, sg_group)
            both.append(
                jnp.concatenate(
                    [
                        c_m[seg, rows, tile * GROUP : (tile + 1) * GROUP]
                        for tile in range(tiles)
                        for seg in range(segments)
                    ],
                    axis=0,
                )
            )
        ordered = mm(perm_ub, jnp.concatenate(both, axis=1)).astype(BF16)
        for n in range(2):
            up_raw[aligned((pair * 2 + n) * PERM_ROWS, PERM_ROWS), :] = ordered[:, n * GROUP : (n + 1) * GROUP]
        return carry

    out_copy = pltpu.make_async_copy(up_raw, out_hbm, out_sem)

    for seg in range(last):
        for k in range(parts - 1):
            back(k, seg).wait_recv()

    def time_backward(t, carry):
        for k in range(parts - 1):
            back_part(k, t).wait_recv()
        rows = aligned(t * TIME_ROWS, TIME_ROWS)
        ordered = []
        for part in range(TIME_ROWS // PERM_ROWS):
            at = aligned(t * per_chunk + part * cg, cg)
            slabs = jnp.concatenate([ret_s[seg, at, :] for seg in range(length)], axis=0)
            ordered.append(mm(perm_tb, slabs).astype(BF16))
        up_b = jnp.concatenate(ordered, axis=0)
        t_sg[rows, :] = up_b
        mg = mm_nt(up_b, tw_ref[3]).astype(BF16)
        q, k, v = t_q[rows, :], t_k[rows, :], t_v[rows, :]
        kT = t_kT[t]
        dq, dk, dv = [], [], []
        for g in range(groups):
            sl = slice(g * GROUP, (g + 1) * GROUP)
            bd, gd = qbd.at[g % slots], gbd.at[g % slots]
            fill_heads(bd, q[sl])
            fill_heads(gd, mg[sl])
            w_b = t_w[t * groups + g]
            w = w_b.astype(F32)
            grad = mm_nt(v[sl], gd[...])
            delta = jnp.sum(w * grad, axis=0, keepdims=True)
            t_b = (w * (grad - delta)).astype(BF16)
            dqT = (LOGIT_SCALE * head_product(kT[:, sl], t_b)).astype(BF16)
            dq.append(dqT.T.astype(F32))
            dk.append(LOGIT_SCALE * mm(t_b, bd[...]))
            dv.append(mm(w_b, gd[...]).astype(BF16))
        qb = head_back(q, t_iq[rows, :], jnp.concatenate(dq, axis=0), blocks)
        kb = head_back(k, t_ik[rows, :], jnp.concatenate(dk, axis=0), blocks)
        vb = jnp.concatenate(dv, axis=0)
        back_s[0, rows, :] = qb
        back_s[1, rows, :] = kb
        back_s[2, rows, :] = vb
        nT = t_nT[t]
        first = t == 0
        for m, back_rows in enumerate((qb, kb, vb)):
            acc_s[m] = mm(nT, back_rows) + jnp.where(first, 0.0, acc_s[m])
        acc_s[3] = mm(t_mT[t], up_b) + jnp.where(first, 0.0, acc_s[3])
        pl.when(t == chunks // 2)(functools.partial(finish0, 1))
        return carry

    acc_s[...] = jnp.zeros_like(acc_s)
    lax.fori_loop(0, chunks, time_backward, 0)
    for m in range(matrices):
        put_grad(0, m, acc_s[m])
    start(stage0(0))
    finish1(1)
    lax.fori_loop(0, channels // row_step, project_out, 0)
    finish0(0)
    lax.fori_loop(0, channels // (2 * sg_group), order_out, 0, unroll=True)
    out_copy.start()
    finish2(1)

    def series_back(t, carry):
        rows = aligned(t * TIME_ROWS, TIME_ROWS)
        grad = mm_nt(back_s[0, rows, :], tw_ref[0]) + mm_nt(back_s[1, rows, :], tw_ref[1])
        grad = grad + mm_nt(back_s[2, rows, :], tw_ref[2])
        x = x_s[rows, :].astype(F32)
        t_sg[rows, :] = (t_sg[rows, :].astype(F32) + row_back(x, grad)).astype(BF16)
        return carry

    lax.fori_loop(0, chunks // 2, series_back, 0)
    finish1(0)
    lax.fori_loop(chunks // 2, chunks, series_back, 0)
    grad_copy = pltpu.make_async_copy(t_sg, sgrad_hbm, grad_sem)
    grad_copy.start()
    finish2(0)
    finish3(1, cg_ref)
    finish3(0, tg_ref)

    grad_copy.wait()
    out_copy.wait()
    for k in range(parts - 1):
        for seg in range(segments):
            inward(k, seg).wait_send()
        for seg in range(last):
            back(k, seg).wait_send()
        for t in range(chunks):
            back_part(k, t).wait_send()


SETTLE_PARTS = 4


def settle_kernel(count, *refs):
    sources, results, held = refs[:count], refs[count : 2 * count], refs[2 * count : 3 * count]
    in_sem, out_sem = refs[3 * count :]
    loads, stores = [], []
    for n in range(count):
        step = held[n].shape[0] // SETTLE_PARTS
        for part in range(SETTLE_PARTS):
            rows = pl.ds(part * step, step)
            loads.append(pltpu.make_async_copy(sources[n].at[rows], held[n].at[rows], in_sem.at[n, part]))
            stores.append(pltpu.make_async_copy(held[n].at[rows], results[n].at[rows], out_sem.at[n, part]))
    for load in loads:
        load.start()
    for load, store in zip(loads, stores):
        load.wait()
        store.start()
    for store in stores:
        store.wait()


def settle(*arrays):
    count = len(arrays)
    hbm = pl.BlockSpec(memory_space=pl.ANY)
    return pl.pallas_call(
        functools.partial(settle_kernel, count),
        out_shape=tuple(jax.ShapeDtypeStruct(a.shape, a.dtype) for a in arrays),
        in_specs=[hbm] * count,
        out_specs=(hbm,) * count,
        scratch_shapes=[pltpu.VMEM(a.shape, a.dtype) for a in arrays]
        + [pltpu.SemaphoreType.DMA((count, SETTLE_PARTS))] * 2,
        name="settle",
    )(*arrays)


VMEM_LIMIT = 62 * 1024 * 1024


def shards(series, upstream_grad, time_weights, channel_weights, neighbors):
    parts, dp = lax.axis_size("mp"), lax.axis_size("dp")
    own, length, features = series.shape[1:]
    channels, segments = upstream_grad.shape[1:3]
    blocks_n, near = neighbors.shape
    block = channels // blocks_n
    matrices = time_weights.shape[0]
    total = own * length
    chunks = total // TIME_ROWS
    row_step = min(channels, 512)
    steps = channels // row_step
    slots = 4 if blocks_n <= 4 else 2
    mine = features // parts
    width = features * matrices // dp
    tiles = features // GROUP
    upstream = jnp.swapaxes(upstream_grad.reshape(channels, segments, tiles, GROUP), 1, 2)
    vmem = pl.BlockSpec(memory_space=pltpu.VMEM)
    hbm = pl.BlockSpec(memory_space=pl.ANY)
    dma = lambda *shape: pltpu.SemaphoreType.DMA(shape)
    b16 = lambda *shape: pltpu.VMEM(shape, BF16)
    f32 = lambda *shape: pltpu.VMEM(shape, F32)
    grads = jax.ShapeDtypeStruct((matrices, mine, features), F32)
    per_block = (blocks_n, block, features)
    contributions = f32(blocks_n * near + 1, block, features)
    output, series_grad, time_grads, channel_grads = pl.pallas_call(
        functools.partial(layer_kernel, parts, dp, length),
        out_shape=(
            jax.ShapeDtypeStruct((channels * segments * tiles, GROUP), BF16),
            jax.ShapeDtypeStruct((total, features), BF16),
            grads,
            grads,
        ),
        in_specs=[pl.BlockSpec(memory_space=pltpu.SMEM), hbm, hbm, vmem, vmem],
        out_specs=(hbm, hbm, vmem, vmem),
        scratch_shapes=[
            b16(total, features),
            b16(channels * segments * tiles, GROUP),
            b16(segments, channels, features),
            b16(length, own, features),
            b16(segments, channels, features),
            b16(segments, channels, features),
            b16(length, own, features),
            b16(chunks, features, TIME_ROWS),
            b16(total, features),
            b16(total, features),
            b16(chunks, features, TIME_ROWS),
            b16(total, features),
            f32(total, features),
            f32(total, features),
            b16(total // GROUP, GROUP, HEADS * GROUP),
            b16(chunks, features, TIME_ROWS),
            b16(total, features),
            b16(3, total, features),
            b16(*per_block),
            b16(*per_block),
            b16(*per_block),
            b16(*per_block),
            b16(blocks_n, features, block),
            b16(blocks_n, features, block),
            f32(*per_block),
            f32(*per_block),
            b16(*per_block),
            contributions,
            contributions,
            b16(segments, channels, features),
            b16(segments, blocks_n, features, block),
            b16(segments, steps, features, row_step),
            b16(slots, HEADS * GROUP, features),
            b16(slots, HEADS * GROUP, features),
            f32(GROUP, GROUP),
            f32(matrices, features, features),
            b16(2, 2, dp // 2, features, width),
            b16(2, dp // 2, features, width),
            b16(2, dp // 2, features, width),
            b16(2, dp // 2 - 1, features, width),
            b16(2, parts, mine, width),
            b16(2, parts - 1, mine, width),
            b16(2, mine, width),
            b16(2, dp, mine, width),
            dma(chunks), pltpu.SemaphoreType.DMA, pltpu.SemaphoreType.DMA, pltpu.SemaphoreType.DMA,
            dma(parts - 1, segments), dma(parts - 1, segments),
            dma(parts - 1, segments), dma(parts - 1, segments),
            dma(parts - 1, chunks), dma(parts - 1, chunks),
            dma(2), dma(2), dma(2, dp // 2 - 1), dma(2, dp // 2 - 1), dma(2, parts - 1), dma(2, parts - 1), dma(2, dp - 1), dma(2, dp - 1),
        ],
        compiler_params=pltpu.CompilerParams(
            vmem_limit_bytes=VMEM_LIMIT, collective_id=0, has_side_effects=True
        ),
        name="layer",
    )(
        neighbors,
        series.reshape(total, features),
        upstream.reshape(channels * segments * tiles, GROUP),
        time_weights,
        channel_weights,
    )
    output, series_grad, time_grads, channel_grads = settle(output, series_grad, time_grads, channel_grads)
    output = jnp.swapaxes(output.reshape(channels, tiles, segments, GROUP), 1, 2)
    return (
        output.reshape(upstream_grad.shape),
        series_grad.reshape(series.shape),
        time_grads,
        channel_grads,
    )


def solution(mesh):
    placed = (P("dp", "mp", None, None), P("dp", None, "mp", None), P(), P(), P())
    return jax.shard_map(
        shards,
        mesh=mesh,
        in_specs=placed,
        out_specs=(
            P("dp", None, "mp", None),
            P("dp", "mp", None, None),
            P(None, "mp", None),
            P(None, "mp", None),
        ),
        check_vma=False,
    )
```

```python
import functools

import jax
import jax.numpy as jnp
from jax import lax
from jax.experimental import pallas as pl
from jax.experimental.pallas import tpu as pltpu
from jax.sharding import PartitionSpec as P

HEADS = 4
EPS = 1e-06
LOGIT_SCALE = 0.25
EXP2_SCALE = LOGIT_SCALE * 1.4426950408889634
GROUP = 128
TIME_ROWS = 512
PERM_ROWS = 256

F32 = jnp.float32
BF16 = jnp.bfloat16
MESH = pl.DeviceIdType.MESH


def mm(a, b):
    return lax.dot_general(a, b, (((1,), (0,)), ((), ())), preferred_element_type=F32)


def mm_nt(a, b):
    return lax.dot_general(a, b, (((1,), (1,)), ((), ())), preferred_element_type=F32)


def iota(shape, dim):
    return lax.broadcasted_iota(jnp.int32, shape, dim)


def eye(size):
    return jnp.where(iota((size, size), 0) == iota((size, size), 1), 1.0, 0.0).astype(BF16)


def regroup(outer, inner):
    size = outer * inner
    row, col = iota((size, size), 0), iota((size, size), 1)
    source = lax.rem(row, outer) * inner + row // outer
    return jnp.where(col == source, 1.0, 0.0).astype(BF16)


def head_blocks(features):
    width = features // HEADS
    rows = iota((features, features), 0) // width
    cols = iota((features, features), 1) // width
    return jnp.where(rows == cols, 1.0 / width, 0.0).astype(BF16)


def inv_rms(values):
    return lax.rsqrt(jnp.mean(values * values, axis=-1, keepdims=True) + EPS)


def head_hat(raw, blocks):
    inv = lax.rsqrt(mm((raw * raw).astype(BF16), blocks) + EPS)
    return (raw * inv).astype(BF16), inv


def head_back(hat_b, inv, grad, blocks):
    hat = hat_b.astype(F32)
    return (inv * (grad - hat * mm((hat * grad).astype(BF16), blocks))).astype(BF16)


def row_back(rows, grad):
    inv = inv_rms(rows)
    hat = rows * inv
    return inv * (grad - hat * jnp.mean(hat * grad, axis=-1, keepdims=True))


def fill_heads(ref, rows):
    width = rows.shape[1] // HEADS
    per_tile = GROUP // width
    tile_head = iota((GROUP, GROUP), 1) // width
    for h in range(HEADS):
        lanes = slice((h // per_tile) * GROUP, (h // per_tile + 1) * GROUP)
        keep = jnp.where(tile_head == h % per_tile, 1.0, 0.0).astype(BF16)
        ref[h * GROUP : (h + 1) * GROUP, lanes] = rows[:, lanes] * keep


def head_product(features_by_keys, keys_by_queries):
    features = features_by_keys.shape[0]
    width = features // HEADS
    per_tile = GROUP // width
    parts = []
    for tile in range(features // GROUP):
        cols = slice(tile * per_tile * GROUP, (tile + 1) * per_tile * GROUP)
        both = mm(features_by_keys[tile * GROUP : (tile + 1) * GROUP, :], keys_by_queries[:, cols])
        for h in range(per_tile):
            parts.append(both[h * width : (h + 1) * width, h * GROUP : (h + 1) * GROUP])
    return jnp.concatenate(parts, axis=0)


def others(axis, size):
    me = lax.axis_index(axis)
    return [lax.rem(me + k, size) for k in range(1, size)]


def aligned(start, size):
    return pl.ds(pl.multiple_of(start, size), size)


def layer_kernel(
    parts, dp, length,
    nb_ref, x_hbm, up_hbm, tw_ref, cw_ref,
    out_hbm, sgrad_hbm, tg_ref, cg_ref,
    x_s, up_raw, up_s, stream_s, cols_s, sg_s, ret_s,
    t_nT, t_q, t_k, t_kT, t_v, t_iq, t_ik, t_w, t_mT, t_sg, back_s,
    c_q, c_k, c_v, c_g, c_kT, c_vT, c_iq, c_ik, c_dq, c_dk, c_dv, c_m, c_mT, c_nT,
    qbd, gbd, tile_keep, acc_s, all_s, core_in, chip_s, dp_in, mp_mine, mp_in, done_s, done_in,
    x_sem, up_sem, out_sem, grad_sem, in_send, in_recv, back_send, back_recv, last_send, last_recv,
    send0, recv0, send1, recv1, send2, recv2, send3, recv3,
):
    segments, channels, features = up_s.shape
    own = stream_s.shape[1]
    rows_total = x_s.shape[0]
    chunks = rows_total // TIME_ROWS
    per_chunk = TIME_ROWS // length
    groups = TIME_ROWS // GROUP
    blocks_n, near = nb_ref.shape
    block = channels // blocks_n
    slots = qbd.shape[0]
    me = lax.axis_index("mp")
    me_dp = lax.axis_index("dp")
    peers = others("mp", parts)
    dp_peers = others("dp", dp)

    def load_x(t):
        return pltpu.make_async_copy(
            x_hbm.at[aligned(t * TIME_ROWS, TIME_ROWS)], x_s.at[aligned(t * TIME_ROWS, TIME_ROWS)], x_sem.at[t]
        )

    def load_up():
        return pltpu.make_async_copy(up_hbm, up_raw, up_sem)

    for t in range(chunks):
        load_x(t).start()
    load_up().start()

    barrier = pltpu.get_barrier_semaphore()
    for peer in peers:
        pl.semaphore_signal(barrier, inc=1, device_id={"mp": peer}, device_id_type=MESH)
    for peer in dp_peers:
        pl.semaphore_signal(barrier, inc=1, device_id={"dp": peer}, device_id_type=MESH)

    blocks = head_blocks(features)
    cg = PERM_ROWS // length
    perm_t = regroup(cg, length)
    perm_tb = regroup(length, cg)
    tiles = features // GROUP
    sg_group = PERM_ROWS // (tiles * segments)
    qbd[...] = jnp.zeros_like(qbd)
    gbd[...] = jnp.zeros_like(gbd)
    tile_keep[...] = jnp.where(
        iota((GROUP, GROUP), 0) // length == iota((GROUP, GROUP), 1) // length, 1.0, 0.0
    ).astype(F32)
    c_dk[blocks_n * near] = jnp.zeros((block, features), F32)
    c_dv[blocks_n * near] = jnp.zeros((block, features), F32)

    def inward(k, seg):
        return pltpu.make_async_remote_copy(
            src_ref=stream_s.at[peers[k] * segments + seg],
            dst_ref=cols_s.at[seg, aligned(me * own, own)],
            send_sem=in_send.at[k, seg],
            recv_sem=in_recv.at[k, seg],
            device_id={"mp": peers[k]},
            device_id_type=MESH,
        )

    def inward_part(k, seg, t):
        return pltpu.make_async_remote_copy(
            src_ref=stream_s.at[peers[k] * segments + seg, aligned(t * per_chunk, per_chunk)],
            dst_ref=cols_s.at[seg, aligned(me * own + t * per_chunk, per_chunk)],
            send_sem=in_send.at[k, seg],
            recv_sem=in_recv.at[k, seg],
            device_id={"mp": peers[k]},
            device_id_type=MESH,
        )

    def back(k, seg):
        return pltpu.make_async_remote_copy(
            src_ref=sg_s.at[seg, aligned(peers[k] * own, own)],
            dst_ref=ret_s.at[me * segments + seg],
            send_sem=back_send.at[k, seg],
            recv_sem=back_recv.at[k, seg],
            device_id={"mp": peers[k]},
            device_id_type=MESH,
        )

    late = min(2, segments)
    first_late = segments - late

    def back_part(k, n, t):
        seg = first_late + n
        return pltpu.make_async_remote_copy(
            src_ref=sg_s.at[seg, aligned(peers[k] * own + t * per_chunk, per_chunk)],
            dst_ref=ret_s.at[me * segments + seg, aligned(t * per_chunk, per_chunk)],
            send_sem=last_send.at[k, n, t],
            recv_sem=last_recv.at[k, n, t],
            device_id={"mp": peers[k]},
            device_id_type=MESH,
        )

    def time_forward(t, carry):
        load_x(t).wait()
        rows = aligned(t * TIME_ROWS, TIME_ROWS)
        x = x_s[rows, :].astype(F32)
        normed = (x * inv_rms(x)).astype(BF16)
        t_nT[t] = normed.T
        q, iq = head_hat(mm(normed, tw_ref[0]), blocks)
        k, ik = head_hat(mm(normed, tw_ref[1]), blocks)
        v = mm(normed, tw_ref[2]).astype(BF16)
        t_q[rows, :], t_k[rows, :], t_v[rows, :] = q, k, v
        t_iq[rows, :], t_ik[rows, :] = iq, ik
        t_kT[t] = k.T
        vT = v.T
        keep = jnp.concatenate([tile_keep[...]] * HEADS, axis=1)
        mixed = []
        for g in range(groups):
            sl = slice(g * GROUP, (g + 1) * GROUP)
            bd = qbd.at[g % slots]
            fill_heads(bd, q[sl])
            e = jnp.exp2(EXP2_SCALE * mm_nt(k[sl], bd[...])) * keep
            w = (e * (1.0 / jnp.sum(e, axis=0, keepdims=True))).astype(BF16)
            t_w[t * groups + g] = w
            mT = head_product(vT[:, sl], w).astype(BF16)
            t_mT[t, :, sl] = mT
            mixed.append(mT.T)
        stream = (x + mm(jnp.concatenate(mixed, axis=0), tw_ref[3])).astype(BF16)
        for part in range(TIME_ROWS // PERM_ROWS):
            ordered = mm(perm_t, stream[part * PERM_ROWS : (part + 1) * PERM_ROWS]).astype(BF16)
            for seg in range(length):
                stream_s[seg, aligned(t * per_chunk + part * cg, cg), :] = ordered[seg * cg : (seg + 1) * cg]
        @pl.when(t == 0)
        def _():
            pl.semaphore_wait(barrier, len(peers) + len(dp_peers))

        for peer in range(parts - 1):
            inward_part(peer, 0, t).start()
        if segments > 1:

            @pl.when(t < chunks // 2)
            def _():
                for peer in range(parts - 1):
                    inward_part(peer, 1, t).start()

        return carry

    lax.fori_loop(0, chunks, time_forward, 0)
    for seg in range(1, segments):
        for k in range(parts - 1):
            if seg == 1:
                for t in range(chunks // 2, chunks):
                    inward_part(k, seg, t).start()
            else:
                inward(k, seg).start()
    for seg in range(segments):
        cols_s[seg, aligned(me * own, own), :] = stream_s[me * segments + seg]

    load_up().wait()
    perm_u = regroup(sg_group, tiles * segments)
    perm_ub = regroup(tiles * segments, sg_group)

    def order_up(pair, carry):
        both = [up_raw[aligned((pair * 2 + n) * PERM_ROWS, PERM_ROWS), :] for n in range(2)]
        ordered = mm(perm_u, jnp.concatenate(both, axis=1)).astype(BF16)
        for n in range(2):
            for tile in range(tiles):
                for seg in range(segments):
                    at = (tile * segments + seg) * sg_group
                    up_s[seg, aligned((pair * 2 + n) * sg_group, sg_group), tile * GROUP : (tile + 1) * GROUP] = ordered[
                        at : at + sg_group, n * GROUP : (n + 1) * GROUP
                    ]
        return carry

    lax.fori_loop(0, channels // (2 * sg_group), order_up, 0, unroll=True)

    row_step = min(channels, 512)
    step_blocks = row_step // block

    def one_segment(seg, carry):
        for k in range(parts - 1):
            inward(k, seg).wait_recv()

        def project(r, inner):
            rows = aligned(r * row_step, row_step)
            these = pl.ds(r * step_blocks, step_blocks)
            x = cols_s[seg, rows, :].astype(F32)
            normed = (x * inv_rms(x)).astype(BF16)
            c_nT[seg, r] = normed.T
            q, iq = head_hat(mm(normed, cw_ref[0]), blocks)
            k, ik = head_hat(mm(normed, cw_ref[1]), blocks)
            v = mm(normed, cw_ref[2]).astype(BF16)
            shaped = (step_blocks, block, features)
            c_q[these], c_k[these], c_v[these] = q.reshape(shaped), k.reshape(shaped), v.reshape(shaped)
            c_iq[these], c_ik[these] = iq.reshape(shaped), ik.reshape(shaped)
            kT = k.T
            vT = v.T
            for b in range(step_blocks):
                c_kT[r * step_blocks + b] = kT[:, b * block : (b + 1) * block]
                c_vT[r * step_blocks + b] = vT[:, b * block : (b + 1) * block]
            c_g[these] = mm_nt(up_s[seg, rows, :], cw_ref[3]).astype(BF16).reshape(shaped)
            return inner

        lax.fori_loop(0, channels // row_step, project, 0)

        def attend(pair, inner):
            for slot in range(slots):
                i = pair * slots + slot
                ids = [nb_ref[i, n] for n in range(near)]
                bd, gd = qbd.at[slot], gbd.at[slot]
                fill_heads(bd, c_q[i])
                fill_heads(gd, c_g[i])
                k_near = jnp.concatenate([c_k[j] for j in ids], axis=0)
                v_near = jnp.concatenate([c_v[j] for j in ids], axis=0)
                kT_near = jnp.concatenate([c_kT[j] for j in ids], axis=1)
                vT_near = jnp.concatenate([c_vT[j] for j in ids], axis=1)
                e = jnp.exp2(EXP2_SCALE * mm_nt(k_near, bd[...]))
                w = e * (1.0 / jnp.sum(e, axis=0, keepdims=True))
                w_b = w.astype(BF16)
                grad = mm_nt(v_near, gd[...])
                delta = jnp.sum(w * grad, axis=0, keepdims=True)
                t_b = (w * (grad - delta)).astype(BF16)
                mT = head_product(vT_near, w_b).astype(BF16)
                c_mT[seg, i] = mT
                c_m[seg, aligned(i * block, block), :] = mT.T
                dqT = (LOGIT_SCALE * head_product(kT_near, t_b)).astype(BF16)
                c_dq[i] = dqT.T
                c_dk[pl.ds(i * near, near)] = mm(t_b, bd[...]).reshape(near, block, features)
                c_dv[pl.ds(i * near, near)] = mm(w_b, gd[...]).reshape(near, block, features)
            return inner

        lax.fori_loop(0, blocks_n // slots, attend, 0)

        def finish_block(j):
            def place(i):
                at = blocks_n * near
                for n in range(1, near):
                    at = jnp.where(nb_ref[i, n] == j, i * near + n, at)
                return at

            def more(m, sums):
                at = place(lax.rem(j + m, blocks_n))
                return sums[0] + c_dk[at], sums[1] + c_dv[at]

            sums = (c_dk[j * near], c_dv[j * near])
            if blocks_n <= 4:
                for m in range(1, blocks_n):
                    sums = more(m, sums)
            else:
                sums = lax.fori_loop(1, blocks_n, more, sums)
            rows = aligned(j * block, block)
            qb = head_back(c_q[j], c_iq[j], c_dq[j].astype(F32), blocks)
            kb = head_back(c_k[j], c_ik[j], LOGIT_SCALE * sums[0], blocks)
            vb = sums[1].astype(BF16)
            at_rows = aligned(seg * channels + j * block, block)
            back_s[0, at_rows, :] = qb
            back_s[1, at_rows, :] = kb
            back_s[2, at_rows, :] = vb
            grad = mm_nt(qb, cw_ref[0]) + mm_nt(kb, cw_ref[1]) + mm_nt(vb, cw_ref[2])
            x = cols_s[seg, rows, :].astype(F32)
            sg_s[seg, rows, :] = (up_s[seg, rows, :].astype(F32) + row_back(x, grad)).astype(BF16)

        def finish(group, inner):
            for n in range(slots):
                finish_block(group * slots + n)
            return inner

        lax.fori_loop(0, blocks_n // slots, finish, 0)

        @pl.when(seg < first_late)
        def _():
            for k in range(parts - 1):
                back(k, seg).start()

        if late > 1:

            @pl.when(seg == first_late)
            def _():
                for t in range(chunks // 2):
                    for k in range(parts - 1):
                        back_part(k, 0, t).start()

        ret_s[me * segments + seg] = sg_s[seg, aligned(me * own, own), :]
        return carry

    lax.fori_loop(0, segments, one_segment, 0)
    for t in range(chunks):
        for n in range(late):
            if n < late - 1 and t < chunks // 2:
                continue
            for k in range(parts - 1):
                back_part(k, n, t).start()

    matrices = tw_ref.shape[0]
    width = all_s.shape[4]
    core, chip = lax.rem(me_dp, 2), me_dp // 2
    chips = dp // 2
    chip_peers = [lax.rem(chip + k, chips) for k in range(1, chips)]
    splits = features // width

    def exchange(src, dst, send, recv, device):
        return pltpu.make_async_remote_copy(
            src_ref=src, dst_ref=dst, send_sem=send, recv_sem=recv, device_id=device, device_id_type=MESH
        )

    def put_grad(r, m, value):
        for part in range(splits):
            place = m * splits + part
            all_s[r, place % 2, place // 2] = value[:, part * width : (part + 1) * width].astype(BF16)

    def stage0(r):
        return [exchange(all_s.at[r, 1 - core], core_in.at[r], send0.at[r], recv0.at[r], {"dp": me_dp + 1 - 2 * core})]

    def stage1(r):
        return [
            exchange(chip_s.at[r, p], dp_in.at[r, k], send1.at[r, k], recv1.at[r, k], {"dp": p * 2 + core})
            for k, p in enumerate(chip_peers)
        ]

    def stage2(r):
        return [
            exchange(mp_mine.at[r, p], mp_in.at[r, k], send2.at[r, k], recv2.at[r, k], {"mp": p})
            for k, p in enumerate(peers)
        ]

    def stage3(r):
        return [
            exchange(done_s.at[r], done_in.at[r, me_dp], send3.at[r, k], recv3.at[r, k], {"dp": p})
            for k, p in enumerate(dp_peers)
        ]

    def start(copies):
        for copy in copies:
            copy.start()

    def wait(copies):
        for copy in copies:
            copy.wait()

    def finish0(r):
        wait(stage0(r))
        chip_s[r] = (all_s[r, core].astype(F32) + core_in[r].astype(F32)).astype(BF16)
        start(stage1(r))

    def finish1(r):
        wait(stage1(r))
        total = chip_s[r, chip].astype(F32)
        for k in range(chips - 1):
            total = total + dp_in[r, k].astype(F32)
        mp_mine[r] = total.astype(BF16).reshape(mp_mine.shape[1:])
        start(stage2(r))

    def finish2(r):
        wait(stage2(r))
        total = mp_mine[r, me].astype(F32)
        for k in range(parts - 1):
            total = total + mp_in[r, k].astype(F32)
        done_s[r] = total.astype(BF16)
        start(stage3(r))
        done_in[r, me_dp] = done_s[r]

    def finish3(r, ref):
        wait(stage3(r))
        for m in range(matrices):
            for part in range(splits):
                ref[m, :, part * width : (part + 1) * width] = done_in[r, m * splits + part].astype(F32) / dp

    steps = channels // row_step
    for m in range(matrices):
        total = None
        for seg in range(segments):
            for r in range(steps):
                rows = slice(r * row_step, (r + 1) * row_step)
                if m < 3:
                    term = mm(c_nT[seg, r], back_s[m, seg * channels + r * row_step : seg * channels + (r + 1) * row_step, :])
                else:
                    mT = jnp.concatenate([c_mT[seg, r * step_blocks + b] for b in range(step_blocks)], axis=1)
                    term = mm(mT, up_s[seg, rows, :])
                total = term if total is None else total + term
        put_grad(1, m, total)
    start(stage0(1))


    def project_out(r, carry):
        rows = aligned(r * row_step, row_step)
        for seg in range(segments):
            res = cols_s[seg, rows, :].astype(F32) + mm(c_m[seg, rows, :], cw_ref[3])
            c_m[seg, rows, :] = res.astype(BF16)
        return carry

    def order_out(pair, carry):
        both = []
        for n in range(2):
            rows = aligned((pair * 2 + n) * sg_group, sg_group)
            both.append(
                jnp.concatenate(
                    [
                        c_m[seg, rows, tile * GROUP : (tile + 1) * GROUP]
                        for tile in range(tiles)
                        for seg in range(segments)
                    ],
                    axis=0,
                )
            )
        ordered = mm(perm_ub, jnp.concatenate(both, axis=1)).astype(BF16)
        for n in range(2):
            up_raw[aligned((pair * 2 + n) * PERM_ROWS, PERM_ROWS), :] = ordered[:, n * GROUP : (n + 1) * GROUP]
        return carry

    out_copy = pltpu.make_async_copy(up_raw, out_hbm, out_sem)

    lax.fori_loop(0, channels // row_step, project_out, 0)
    lax.fori_loop(0, channels // (2 * sg_group), order_out, 0, unroll=True)
    out_copy.start()
    finish0(1)
    for seg in range(first_late):
        for k in range(parts - 1):
            back(k, seg).wait_recv()

    def time_backward(t, carry):
        for n in range(late):
            for k in range(parts - 1):
                back_part(k, n, t).wait_recv()
        rows = aligned(t * TIME_ROWS, TIME_ROWS)
        ordered = []
        for part in range(TIME_ROWS // PERM_ROWS):
            at = aligned(t * per_chunk + part * cg, cg)
            slabs = jnp.concatenate([ret_s[seg, at, :] for seg in range(length)], axis=0)
            ordered.append(mm(perm_tb, slabs).astype(BF16))
        up_b = jnp.concatenate(ordered, axis=0)
        t_sg[rows, :] = up_b
        mg = mm_nt(up_b, tw_ref[3]).astype(BF16)
        q, k, v = t_q[rows, :], t_k[rows, :], t_v[rows, :]
        kT = t_kT[t]
        dq, dk, dv = [], [], []
        for g in range(groups):
            sl = slice(g * GROUP, (g + 1) * GROUP)
            bd, gd = qbd.at[g % slots], gbd.at[g % slots]
            fill_heads(bd, q[sl])
            fill_heads(gd, mg[sl])
            w_b = t_w[t * groups + g]
            w = w_b.astype(F32)
            grad = mm_nt(v[sl], gd[...])
            delta = jnp.sum(w * grad, axis=0, keepdims=True)
            t_b = (w * (grad - delta)).astype(BF16)
            dqT = (LOGIT_SCALE * head_product(kT[:, sl], t_b)).astype(BF16)
            dq.append(dqT.T.astype(F32))
            dk.append(LOGIT_SCALE * mm(t_b, bd[...]))
            dv.append(mm(w_b, gd[...]).astype(BF16))
        qb = head_back(q, t_iq[rows, :], jnp.concatenate(dq, axis=0), blocks)
        kb = head_back(k, t_ik[rows, :], jnp.concatenate(dk, axis=0), blocks)
        vb = jnp.concatenate(dv, axis=0)
        back_s[0, rows, :] = qb
        back_s[1, rows, :] = kb
        back_s[2, rows, :] = vb
        nT = t_nT[t]
        first = t == 0
        for m, back_rows in enumerate((qb, kb, vb)):
            acc_s[m] = mm(nT, back_rows) + jnp.where(first, 0.0, acc_s[m])
        acc_s[3] = mm(t_mT[t], up_b) + jnp.where(first, 0.0, acc_s[3])
        pl.when(t == 0)(functools.partial(finish1, 1))
        return carry

    acc_s[...] = jnp.zeros_like(acc_s)
    lax.fori_loop(0, chunks, time_backward, 0)
    for m in range(matrices):
        put_grad(0, m, acc_s[m])
    start(stage0(0))
    finish2(1)

    def series_back(t, carry):
        rows = aligned(t * TIME_ROWS, TIME_ROWS)
        grad = mm_nt(back_s[0, rows, :], tw_ref[0]) + mm_nt(back_s[1, rows, :], tw_ref[1])
        grad = grad + mm_nt(back_s[2, rows, :], tw_ref[2])
        x = x_s[rows, :].astype(F32)
        t_sg[rows, :] = (t_sg[rows, :].astype(F32) + row_back(x, grad)).astype(BF16)
        return carry

    lax.fori_loop(0, chunks // 4, series_back, 0)
    finish0(0)
    lax.fori_loop(chunks // 4, chunks, series_back, 0)
    finish1(0)
    grad_copy = pltpu.make_async_copy(t_sg, sgrad_hbm, grad_sem)
    grad_copy.start()
    finish3(1, cg_ref)
    finish2(0)
    finish3(0, tg_ref)

    grad_copy.wait()
    out_copy.wait()
    for k in range(parts - 1):
        for seg in range(segments):
            inward(k, seg).wait_send()
        for seg in range(first_late):
            back(k, seg).wait_send()
        for t in range(chunks):
            for n in range(late):
                back_part(k, n, t).wait_send()


SETTLE_PARTS = 4


def settle_kernel(count, *refs):
    sources, results, held = refs[:count], refs[count : 2 * count], refs[2 * count : 3 * count]
    in_sem, out_sem = refs[3 * count :]
    loads, stores = [], []
    for n in range(count):
        step = held[n].shape[0] // SETTLE_PARTS
        for part in range(SETTLE_PARTS):
            rows = pl.ds(part * step, step)
            loads.append(pltpu.make_async_copy(sources[n].at[rows], held[n].at[rows], in_sem.at[n, part]))
            stores.append(pltpu.make_async_copy(held[n].at[rows], results[n].at[rows], out_sem.at[n, part]))
    for load in loads:
        load.start()
    for load, store in zip(loads, stores):
        load.wait()
        store.start()
    for store in stores:
        store.wait()


def settle(*arrays):
    count = len(arrays)
    hbm = pl.BlockSpec(memory_space=pl.ANY)
    return pl.pallas_call(
        functools.partial(settle_kernel, count),
        out_shape=tuple(jax.ShapeDtypeStruct(a.shape, a.dtype) for a in arrays),
        in_specs=[hbm] * count,
        out_specs=(hbm,) * count,
        scratch_shapes=[pltpu.VMEM(a.shape, a.dtype) for a in arrays]
        + [pltpu.SemaphoreType.DMA((count, SETTLE_PARTS))] * 2,
        name="settle",
    )(*arrays)


VMEM_LIMIT = 62 * 1024 * 1024


def shards(series, upstream_grad, time_weights, channel_weights, neighbors):
    parts, dp = lax.axis_size("mp"), lax.axis_size("dp")
    own, length, features = series.shape[1:]
    channels, segments = upstream_grad.shape[1:3]
    blocks_n, near = neighbors.shape
    block = channels // blocks_n
    matrices = time_weights.shape[0]
    total = own * length
    chunks = total // TIME_ROWS
    row_step = min(channels, 512)
    steps = channels // row_step
    slots = 4 if blocks_n <= 4 else 2
    mine = features // parts
    width = features * matrices // dp
    tiles = features // GROUP
    upstream = jnp.swapaxes(upstream_grad.reshape(channels, segments, tiles, GROUP), 1, 2)
    vmem = pl.BlockSpec(memory_space=pltpu.VMEM)
    hbm = pl.BlockSpec(memory_space=pl.ANY)
    dma = lambda *shape: pltpu.SemaphoreType.DMA(shape)
    b16 = lambda *shape: pltpu.VMEM(shape, BF16)
    f32 = lambda *shape: pltpu.VMEM(shape, F32)
    grads = jax.ShapeDtypeStruct((matrices, mine, features), F32)
    per_block = (blocks_n, block, features)
    contributions = f32(blocks_n * near + 1, block, features)
    output, series_grad, time_grads, channel_grads = pl.pallas_call(
        functools.partial(layer_kernel, parts, dp, length),
        out_shape=(
            jax.ShapeDtypeStruct((channels * segments * tiles, GROUP), BF16),
            jax.ShapeDtypeStruct((total, features), BF16),
            grads,
            grads,
        ),
        in_specs=[pl.BlockSpec(memory_space=pltpu.SMEM), hbm, hbm, vmem, vmem],
        out_specs=(hbm, hbm, vmem, vmem),
        scratch_shapes=[
            b16(total, features),
            b16(channels * segments * tiles, GROUP),
            b16(segments, channels, features),
            b16(length, own, features),
            b16(segments, channels, features),
            b16(segments, channels, features),
            b16(length, own, features),
            b16(chunks, features, TIME_ROWS),
            b16(total, features),
            b16(total, features),
            b16(chunks, features, TIME_ROWS),
            b16(total, features),
            f32(total, features),
            f32(total, features),
            b16(total // GROUP, GROUP, HEADS * GROUP),
            b16(chunks, features, TIME_ROWS),
            b16(total, features),
            b16(3, total, features),
            b16(*per_block),
            b16(*per_block),
            b16(*per_block),
            b16(*per_block),
            b16(blocks_n, features, block),
            b16(blocks_n, features, block),
            f32(*per_block),
            f32(*per_block),
            b16(*per_block),
            contributions,
            contributions,
            b16(segments, channels, features),
            b16(segments, blocks_n, features, block),
            b16(segments, steps, features, row_step),
            b16(slots, HEADS * GROUP, features),
            b16(slots, HEADS * GROUP, features),
            f32(GROUP, GROUP),
            f32(matrices, features, features),
            b16(2, 2, dp // 2, features, width),
            b16(2, dp // 2, features, width),
            b16(2, dp // 2, features, width),
            b16(2, dp // 2 - 1, features, width),
            b16(2, parts, mine, width),
            b16(2, parts - 1, mine, width),
            b16(2, mine, width),
            b16(2, dp, mine, width),
            dma(chunks), pltpu.SemaphoreType.DMA, pltpu.SemaphoreType.DMA, pltpu.SemaphoreType.DMA,
            dma(parts - 1, segments), dma(parts - 1, segments),
            dma(parts - 1, segments), dma(parts - 1, segments),
            dma(parts - 1, min(2, segments), chunks), dma(parts - 1, min(2, segments), chunks),
            dma(2), dma(2), dma(2, dp // 2 - 1), dma(2, dp // 2 - 1), dma(2, parts - 1), dma(2, parts - 1), dma(2, dp - 1), dma(2, dp - 1),
        ],
        compiler_params=pltpu.CompilerParams(
            vmem_limit_bytes=VMEM_LIMIT, collective_id=0, has_side_effects=True
        ),
        name="layer",
    )(
        neighbors,
        series.reshape(total, features),
        upstream.reshape(channels * segments * tiles, GROUP),
        time_weights,
        channel_weights,
    )
    output, series_grad, time_grads, channel_grads = settle(output, series_grad, time_grads, channel_grads)
    output = jnp.swapaxes(output.reshape(channels, tiles, segments, GROUP), 1, 2)
    return (
        output.reshape(upstream_grad.shape),
        series_grad.reshape(series.shape),
        time_grads,
        channel_grads,
    )


def solution(mesh):
    placed = (P("dp", "mp", None, None), P("dp", None, "mp", None), P(), P(), P())
    return jax.shard_map(
        shards,
        mesh=mesh,
        in_specs=placed,
        out_specs=(
            P("dp", None, "mp", None),
            P("dp", "mp", None, None),
            P(None, "mp", None),
            P(None, "mp", None),
        ),
        check_vma=False,
    )
```

```python
import functools

import jax
import jax.numpy as jnp
from jax import lax
from jax.experimental import pallas as pl
from jax.experimental.pallas import tpu as pltpu
from jax.sharding import PartitionSpec as P

HEADS = 4
EPS = 1e-06
LOGIT_SCALE = 0.25
EXP2_SCALE = LOGIT_SCALE * 1.4426950408889634
GROUP = 128
TIME_ROWS = 512
PERM_ROWS = 256

F32 = jnp.float32
BF16 = jnp.bfloat16
MESH = pl.DeviceIdType.MESH


def mm(a, b):
    return lax.dot_general(a, b, (((1,), (0,)), ((), ())), preferred_element_type=F32)


def mm_nt(a, b):
    return lax.dot_general(a, b, (((1,), (1,)), ((), ())), preferred_element_type=F32)


def iota(shape, dim):
    return lax.broadcasted_iota(jnp.int32, shape, dim)


def eye(size):
    return jnp.where(iota((size, size), 0) == iota((size, size), 1), 1.0, 0.0).astype(BF16)


def regroup(outer, inner):
    size = outer * inner
    row, col = iota((size, size), 0), iota((size, size), 1)
    source = lax.rem(row, outer) * inner + row // outer
    return jnp.where(col == source, 1.0, 0.0).astype(BF16)


def head_blocks(features):
    width = features // HEADS
    rows = iota((features, features), 0) // width
    cols = iota((features, features), 1) // width
    return jnp.where(rows == cols, 1.0 / width, 0.0).astype(BF16)


def inv_rms(values):
    return lax.rsqrt(jnp.mean(values * values, axis=-1, keepdims=True) + EPS)


def head_hat(raw, blocks):
    inv = lax.rsqrt(mm((raw * raw).astype(BF16), blocks) + EPS)
    return (raw * inv).astype(BF16), inv


def head_back(hat_b, inv, grad, blocks):
    hat = hat_b.astype(F32)
    return (inv * (grad - hat * mm((hat * grad).astype(BF16), blocks))).astype(BF16)


def row_back(rows, grad):
    inv = inv_rms(rows)
    hat = rows * inv
    return inv * (grad - hat * jnp.mean(hat * grad, axis=-1, keepdims=True))


def fill_heads(ref, rows):
    width = rows.shape[1] // HEADS
    per_tile = GROUP // width
    tile_head = iota((GROUP, GROUP), 1) // width
    for h in range(HEADS):
        lanes = slice((h // per_tile) * GROUP, (h // per_tile + 1) * GROUP)
        keep = jnp.where(tile_head == h % per_tile, 1.0, 0.0).astype(BF16)
        ref[h * GROUP : (h + 1) * GROUP, lanes] = rows[:, lanes] * keep


def head_product(features_by_keys, keys_by_queries):
    features = features_by_keys.shape[0]
    width = features // HEADS
    per_tile = GROUP // width
    parts = []
    for tile in range(features // GROUP):
        cols = slice(tile * per_tile * GROUP, (tile + 1) * per_tile * GROUP)
        both = mm(features_by_keys[tile * GROUP : (tile + 1) * GROUP, :], keys_by_queries[:, cols])
        for h in range(per_tile):
            parts.append(both[h * width : (h + 1) * width, h * GROUP : (h + 1) * GROUP])
    return jnp.concatenate(parts, axis=0)


def others(axis, size):
    me = lax.axis_index(axis)
    return [lax.rem(me + k, size) for k in range(1, size)]


def aligned(start, size):
    return pl.ds(pl.multiple_of(start, size), size)


def layer_kernel(
    parts, dp, length,
    nb_ref, x_hbm, up_hbm, tw_hbm, cw_hbm,
    out_hbm, sgrad_hbm, tg_ref, cg_ref,
    tw_ref, cw_ref, x_s, up_raw, up_s, stream_s, cols_s, sg_s, ret_s,
    t_nT, t_q, t_k, t_kT, t_v, t_iq, t_ik, t_w, t_mT, t_sg, back_s,
    c_q, c_k, c_v, c_g, c_kT, c_vT, c_iq, c_ik, c_dq, c_dk, c_dv, c_m, c_mT, c_nT,
    qbd, gbd, tile_keep, acc_s, all_s, core_in, chip_s, dp_in, mp_mine, mp_in, done_s, done_in,
    w_sem, x_sem, up_sem, out_sem, grad_sem, in_send, in_recv, back_send, back_recv, last_send, last_recv,
    send0, recv0, send1, recv1, send2, recv2, send3, recv3,
):
    segments, channels, features = up_s.shape
    own = stream_s.shape[1]
    rows_total = x_s.shape[0]
    chunks = rows_total // TIME_ROWS
    per_chunk = TIME_ROWS // length
    groups = TIME_ROWS // GROUP
    blocks_n, near = nb_ref.shape
    block = channels // blocks_n
    slots = qbd.shape[0]
    me = lax.axis_index("mp")
    me_dp = lax.axis_index("dp")
    peers = others("mp", parts)
    if parts == 4:
        peers = [lax.rem(me + 2, 4), 3 - me, me + 1 - 2 * lax.rem(me, 2)]
    dp_peers = others("dp", dp)

    def load_x(t):
        return pltpu.make_async_copy(
            x_hbm.at[aligned(t * TIME_ROWS, TIME_ROWS)], x_s.at[aligned(t * TIME_ROWS, TIME_ROWS)], x_sem.at[t]
        )

    def load_up():
        return pltpu.make_async_copy(up_hbm, up_raw, up_sem)

    load_weights = [
        pltpu.make_async_copy(tw_hbm, tw_ref, w_sem.at[0]),
        pltpu.make_async_copy(cw_hbm, cw_ref, w_sem.at[1]),
    ]
    load_x(0).start()
    load_weights[0].start()
    for t in range(1, chunks):
        load_x(t).start()
    load_weights[1].start()
    load_up().start()

    barrier = pltpu.get_barrier_semaphore()
    for peer in peers:
        pl.semaphore_signal(barrier, inc=1, device_id={"mp": peer}, device_id_type=MESH)
    for peer in dp_peers:
        pl.semaphore_signal(barrier, inc=1, device_id={"dp": peer}, device_id_type=MESH)

    blocks = head_blocks(features)
    cg = PERM_ROWS // length
    perm_t = regroup(cg, length)
    perm_tb = regroup(length, cg)
    tiles = features // GROUP
    sg_group = PERM_ROWS // (tiles * segments)
    qbd[...] = jnp.zeros_like(qbd)
    gbd[...] = jnp.zeros_like(gbd)
    tile_keep[...] = jnp.where(
        iota((GROUP, GROUP), 0) // length == iota((GROUP, GROUP), 1) // length, 1.0, 0.0
    ).astype(F32)
    c_dk[blocks_n * near] = jnp.zeros((block, features), F32)
    c_dv[blocks_n * near] = jnp.zeros((block, features), F32)

    load_weights[0].wait()

    def inward(k, seg):
        return pltpu.make_async_remote_copy(
            src_ref=stream_s.at[peers[k] * segments + seg],
            dst_ref=cols_s.at[seg, aligned(me * own, own)],
            send_sem=in_send.at[k, seg],
            recv_sem=in_recv.at[k, seg],
            device_id={"mp": peers[k]},
            device_id_type=MESH,
        )

    def inward_part(k, seg, t):
        return pltpu.make_async_remote_copy(
            src_ref=stream_s.at[peers[k] * segments + seg, aligned(t * per_chunk, per_chunk)],
            dst_ref=cols_s.at[seg, aligned(me * own + t * per_chunk, per_chunk)],
            send_sem=in_send.at[k, seg],
            recv_sem=in_recv.at[k, seg],
            device_id={"mp": peers[k]},
            device_id_type=MESH,
        )

    def back(k, seg):
        return pltpu.make_async_remote_copy(
            src_ref=sg_s.at[seg, aligned(peers[k] * own, own)],
            dst_ref=ret_s.at[me * segments + seg],
            send_sem=back_send.at[k, seg],
            recv_sem=back_recv.at[k, seg],
            device_id={"mp": peers[k]},
            device_id_type=MESH,
        )

    late = min(2, segments)
    first_late = segments - late

    def back_part(k, n, t):
        seg = first_late + n
        return pltpu.make_async_remote_copy(
            src_ref=sg_s.at[seg, aligned(peers[k] * own + t * per_chunk, per_chunk)],
            dst_ref=ret_s.at[me * segments + seg, aligned(t * per_chunk, per_chunk)],
            send_sem=last_send.at[k, n, t],
            recv_sem=last_recv.at[k, n, t],
            device_id={"mp": peers[k]},
            device_id_type=MESH,
        )

    def time_forward(t, carry):
        load_x(t).wait()
        rows = aligned(t * TIME_ROWS, TIME_ROWS)
        x = x_s[rows, :].astype(F32)
        normed = (x * inv_rms(x)).astype(BF16)
        t_nT[t] = normed.T
        q, iq = head_hat(mm(normed, tw_ref[0]), blocks)
        k, ik = head_hat(mm(normed, tw_ref[1]), blocks)
        v = mm(normed, tw_ref[2]).astype(BF16)
        t_q[rows, :], t_k[rows, :], t_v[rows, :] = q, k, v
        t_iq[rows, :], t_ik[rows, :] = iq, ik
        t_kT[t] = k.T
        vT = v.T
        keep = jnp.concatenate([tile_keep[...]] * HEADS, axis=1)
        mixed = []
        for g in range(groups):
            sl = slice(g * GROUP, (g + 1) * GROUP)
            bd = qbd.at[g % slots]
            fill_heads(bd, q[sl])
            e = jnp.exp2(EXP2_SCALE * mm_nt(k[sl], bd[...])) * keep
            w = (e * (1.0 / jnp.sum(e, axis=0, keepdims=True))).astype(BF16)
            t_w[t * groups + g] = w
            mT = head_product(vT[:, sl], w).astype(BF16)
            t_mT[t, :, sl] = mT
            mixed.append(mT.T)
        stream = (x + mm(jnp.concatenate(mixed, axis=0), tw_ref[3])).astype(BF16)
        for part in range(TIME_ROWS // PERM_ROWS):
            ordered = mm(perm_t, stream[part * PERM_ROWS : (part + 1) * PERM_ROWS]).astype(BF16)
            for seg in range(length):
                stream_s[seg, aligned(t * per_chunk + part * cg, cg), :] = ordered[seg * cg : (seg + 1) * cg]
        @pl.when(t == 0)
        def _():
            pl.semaphore_wait(barrier, len(peers) + len(dp_peers))

        for peer in range(parts - 1):
            inward_part(peer, 0, t).start()
        if segments > 1:

            @pl.when(t < chunks // 2)
            def _():
                for peer in range(parts - 1):
                    inward_part(peer, 1, t).start()

        return carry

    lax.fori_loop(0, chunks, time_forward, 0)
    for seg in range(1, segments):
        for k in range(parts - 1):
            if seg == 1:
                for t in range(chunks // 2, chunks):
                    inward_part(k, seg, t).start()
            else:
                inward(k, seg).start()
    for seg in range(segments):
        cols_s[seg, aligned(me * own, own), :] = stream_s[me * segments + seg]

    load_up().wait()
    load_weights[1].wait()
    perm_u = regroup(sg_group, tiles * segments)
    perm_ub = regroup(tiles * segments, sg_group)

    def order_up(pair, carry):
        both = [up_raw[aligned((pair * 2 + n) * PERM_ROWS, PERM_ROWS), :] for n in range(2)]
        ordered = mm(perm_u, jnp.concatenate(both, axis=1)).astype(BF16)
        for n in range(2):
            for tile in range(tiles):
                for seg in range(segments):
                    at = (tile * segments + seg) * sg_group
                    up_s[seg, aligned((pair * 2 + n) * sg_group, sg_group), tile * GROUP : (tile + 1) * GROUP] = ordered[
                        at : at + sg_group, n * GROUP : (n + 1) * GROUP
                    ]
        return carry

    lax.fori_loop(0, channels // (2 * sg_group), order_up, 0, unroll=True)

    row_step = min(channels, 512)
    step_blocks = row_step // block

    def one_segment(seg, carry):
        for k in range(parts - 1):
            inward(k, seg).wait_recv()

        def project(r, inner):
            rows = aligned(r * row_step, row_step)
            these = pl.ds(r * step_blocks, step_blocks)
            x = cols_s[seg, rows, :].astype(F32)
            normed = (x * inv_rms(x)).astype(BF16)
            c_nT[seg, r] = normed.T
            q, iq = head_hat(mm(normed, cw_ref[0]), blocks)
            k, ik = head_hat(mm(normed, cw_ref[1]), blocks)
            v = mm(normed, cw_ref[2]).astype(BF16)
            shaped = (step_blocks, block, features)
            c_q[these], c_k[these], c_v[these] = q.reshape(shaped), k.reshape(shaped), v.reshape(shaped)
            c_iq[these], c_ik[these] = iq.reshape(shaped), ik.reshape(shaped)
            kT = k.T
            vT = v.T
            for b in range(step_blocks):
                c_kT[r * step_blocks + b] = kT[:, b * block : (b + 1) * block]
                c_vT[r * step_blocks + b] = vT[:, b * block : (b + 1) * block]
            c_g[these] = mm_nt(up_s[seg, rows, :], cw_ref[3]).astype(BF16).reshape(shaped)
            return inner

        lax.fori_loop(0, channels // row_step, project, 0)

        def attend(pair, inner):
            for slot in range(slots):
                i = pair * slots + slot
                ids = [nb_ref[i, n] for n in range(near)]
                bd, gd = qbd.at[slot], gbd.at[slot]
                fill_heads(bd, c_q[i])
                fill_heads(gd, c_g[i])
                k_near = jnp.concatenate([c_k[j] for j in ids], axis=0)
                v_near = jnp.concatenate([c_v[j] for j in ids], axis=0)
                kT_near = jnp.concatenate([c_kT[j] for j in ids], axis=1)
                vT_near = jnp.concatenate([c_vT[j] for j in ids], axis=1)
                e = jnp.exp2(EXP2_SCALE * mm_nt(k_near, bd[...]))
                w = e * (1.0 / jnp.sum(e, axis=0, keepdims=True))
                w_b = w.astype(BF16)
                grad = mm_nt(v_near, gd[...])
                delta = jnp.sum(w * grad, axis=0, keepdims=True)
                t_b = (w * (grad - delta)).astype(BF16)
                mT = head_product(vT_near, w_b).astype(BF16)
                c_mT[seg, i] = mT
                c_m[seg, aligned(i * block, block), :] = mT.T
                dqT = (LOGIT_SCALE * head_product(kT_near, t_b)).astype(BF16)
                c_dq[i] = dqT.T
                c_dk[pl.ds(i * near, near)] = mm(t_b, bd[...]).reshape(near, block, features)
                c_dv[pl.ds(i * near, near)] = mm(w_b, gd[...]).reshape(near, block, features)
            return inner

        lax.fori_loop(0, blocks_n // slots, attend, 0)

        def finish_block(j):
            def place(i):
                at = blocks_n * near
                for n in range(1, near):
                    at = jnp.where(nb_ref[i, n] == j, i * near + n, at)
                return at

            def more(m, sums):
                at = place(lax.rem(j + m, blocks_n))
                return sums[0] + c_dk[at], sums[1] + c_dv[at]

            sums = (c_dk[j * near], c_dv[j * near])
            if blocks_n <= 4:
                for m in range(1, blocks_n):
                    sums = more(m, sums)
            else:
                sums = lax.fori_loop(1, blocks_n, more, sums)
            rows = aligned(j * block, block)
            qb = head_back(c_q[j], c_iq[j], c_dq[j].astype(F32), blocks)
            kb = head_back(c_k[j], c_ik[j], LOGIT_SCALE * sums[0], blocks)
            vb = sums[1].astype(BF16)
            at_rows = aligned(seg * channels + j * block, block)
            back_s[0, at_rows, :] = qb
            back_s[1, at_rows, :] = kb
            back_s[2, at_rows, :] = vb
            grad = mm_nt(qb, cw_ref[0]) + mm_nt(kb, cw_ref[1]) + mm_nt(vb, cw_ref[2])
            x = cols_s[seg, rows, :].astype(F32)
            sg_s[seg, rows, :] = (up_s[seg, rows, :].astype(F32) + row_back(x, grad)).astype(BF16)

        def finish(group, inner):
            for n in range(slots):
                finish_block(group * slots + n)
            return inner

        lax.fori_loop(0, blocks_n // slots, finish, 0)

        @pl.when(seg < first_late)
        def _():
            for k in range(parts - 1):
                back(k, seg).start()

        if late > 1:

            @pl.when(seg == first_late)
            def _():
                for t in range(chunks // 2):
                    for k in range(parts - 1):
                        back_part(k, 0, t).start()

        ret_s[me * segments + seg] = sg_s[seg, aligned(me * own, own), :]
        return carry

    lax.fori_loop(0, segments, one_segment, 0)
    for t in range(chunks):
        for n in range(late):
            if n < late - 1 and t < chunks // 2:
                continue
            for k in range(parts - 1):
                back_part(k, n, t).start()

    matrices = tw_ref.shape[0]
    width = all_s.shape[4]
    core, chip = lax.rem(me_dp, 2), me_dp // 2
    chips = dp // 2
    chip_peers = [lax.rem(chip + k, chips) for k in range(1, chips)]
    splits = features // width

    def exchange(src, dst, send, recv, device):
        return pltpu.make_async_remote_copy(
            src_ref=src, dst_ref=dst, send_sem=send, recv_sem=recv, device_id=device, device_id_type=MESH
        )

    def put_grad(r, m, value):
        for part in range(splits):
            place = m * splits + part
            all_s[r, place % 2, place // 2] = value[:, part * width : (part + 1) * width].astype(BF16)

    def stage0(r):
        return [exchange(all_s.at[r, 1 - core], core_in.at[r], send0.at[r], recv0.at[r], {"dp": me_dp + 1 - 2 * core})]

    def stage1(r):
        return [
            exchange(chip_s.at[r, p], dp_in.at[r, k], send1.at[r, k], recv1.at[r, k], {"dp": p * 2 + core})
            for k, p in enumerate(chip_peers)
        ]

    def stage2(r):
        return [
            exchange(mp_mine.at[r, p], mp_in.at[r, k], send2.at[r, k], recv2.at[r, k], {"mp": p})
            for k, p in enumerate(peers)
        ]

    def stage3(r):
        return [
            exchange(done_s.at[r], done_in.at[r, me_dp], send3.at[r, k], recv3.at[r, k], {"dp": p})
            for k, p in enumerate(dp_peers)
        ]

    def start(copies):
        for copy in copies:
            copy.start()

    def wait(copies):
        for copy in copies:
            copy.wait()

    def finish0(r):
        wait(stage0(r))
        chip_s[r] = (all_s[r, core].astype(F32) + core_in[r].astype(F32)).astype(BF16)
        start(stage1(r))

    def finish1(r):
        wait(stage1(r))
        total = chip_s[r, chip].astype(F32)
        for k in range(chips - 1):
            total = total + dp_in[r, k].astype(F32)
        mp_mine[r] = total.astype(BF16).reshape(mp_mine.shape[1:])
        start(stage2(r))

    def finish2(r):
        wait(stage2(r))
        total = mp_mine[r, me].astype(F32)
        for k in range(parts - 1):
            total = total + mp_in[r, k].astype(F32)
        done_s[r] = total.astype(BF16)
        start(stage3(r))
        done_in[r, me_dp] = done_s[r]

    def finish3(r, ref):
        wait(stage3(r))
        for m in range(matrices):
            for part in range(splits):
                ref[m, :, part * width : (part + 1) * width] = done_in[r, m * splits + part].astype(F32) / dp

    steps = channels // row_step
    for m in range(matrices):
        total = None
        for seg in range(segments):
            for r in range(steps):
                rows = slice(r * row_step, (r + 1) * row_step)
                if m < 3:
                    term = mm(c_nT[seg, r], back_s[m, seg * channels + r * row_step : seg * channels + (r + 1) * row_step, :])
                else:
                    mT = jnp.concatenate([c_mT[seg, r * step_blocks + b] for b in range(step_blocks)], axis=1)
                    term = mm(mT, up_s[seg, rows, :])
                total = term if total is None else total + term
        put_grad(1, m, total)
    start(stage0(1))


    def project_out(r, carry):
        rows = aligned(r * row_step, row_step)
        for seg in range(segments):
            res = cols_s[seg, rows, :].astype(F32) + mm(c_m[seg, rows, :], cw_ref[3])
            c_m[seg, rows, :] = res.astype(BF16)
        return carry

    def order_out(pair, carry):
        both = []
        for n in range(2):
            rows = aligned((pair * 2 + n) * sg_group, sg_group)
            both.append(
                jnp.concatenate(
                    [
                        c_m[seg, rows, tile * GROUP : (tile + 1) * GROUP]
                        for tile in range(tiles)
                        for seg in range(segments)
                    ],
                    axis=0,
                )
            )
        ordered = mm(perm_ub, jnp.concatenate(both, axis=1)).astype(BF16)
        for n in range(2):
            up_raw[aligned((pair * 2 + n) * PERM_ROWS, PERM_ROWS), :] = ordered[:, n * GROUP : (n + 1) * GROUP]
        return carry

    out_copy = pltpu.make_async_copy(up_raw, out_hbm, out_sem)

    lax.fori_loop(0, channels // row_step, project_out, 0)
    lax.fori_loop(0, channels // (2 * sg_group), order_out, 0, unroll=True)
    out_copy.start()
    finish0(1)
    for seg in range(first_late):
        for k in range(parts - 1):
            back(k, seg).wait_recv()

    def time_backward(t, carry):
        for n in range(late):
            for k in range(parts - 1):
                back_part(k, n, t).wait_recv()
        rows = aligned(t * TIME_ROWS, TIME_ROWS)
        ordered = []
        for part in range(TIME_ROWS // PERM_ROWS):
            at = aligned(t * per_chunk + part * cg, cg)
            slabs = jnp.concatenate([ret_s[seg, at, :] for seg in range(length)], axis=0)
            ordered.append(mm(perm_tb, slabs).astype(BF16))
        up_b = jnp.concatenate(ordered, axis=0)
        t_sg[rows, :] = up_b
        mg = mm_nt(up_b, tw_ref[3]).astype(BF16)
        q, k, v = t_q[rows, :], t_k[rows, :], t_v[rows, :]
        kT = t_kT[t]
        dq, dk, dv = [], [], []
        for g in range(groups):
            sl = slice(g * GROUP, (g + 1) * GROUP)
            bd, gd = qbd.at[g % slots], gbd.at[g % slots]
            fill_heads(bd, q[sl])
            fill_heads(gd, mg[sl])
            w_b = t_w[t * groups + g]
            w = w_b.astype(F32)
            grad = mm_nt(v[sl], gd[...])
            delta = jnp.sum(w * grad, axis=0, keepdims=True)
            t_b = (w * (grad - delta)).astype(BF16)
            dqT = (LOGIT_SCALE * head_product(kT[:, sl], t_b)).astype(BF16)
            dq.append(dqT.T.astype(F32))
            dk.append(LOGIT_SCALE * mm(t_b, bd[...]))
            dv.append(mm(w_b, gd[...]).astype(BF16))
        qb = head_back(q, t_iq[rows, :], jnp.concatenate(dq, axis=0), blocks)
        kb = head_back(k, t_ik[rows, :], jnp.concatenate(dk, axis=0), blocks)
        vb = jnp.concatenate(dv, axis=0)
        back_s[0, rows, :] = qb
        back_s[1, rows, :] = kb
        back_s[2, rows, :] = vb
        nT = t_nT[t]
        first = t == 0
        for m, back_rows in enumerate((qb, kb, vb)):
            acc_s[m] = mm(nT, back_rows) + jnp.where(first, 0.0, acc_s[m])
        acc_s[3] = mm(t_mT[t], up_b) + jnp.where(first, 0.0, acc_s[3])
        pl.when(t == 0)(functools.partial(finish1, 1))
        return carry

    acc_s[...] = jnp.zeros_like(acc_s)
    lax.fori_loop(0, chunks, time_backward, 0)
    for m in range(matrices):
        put_grad(0, m, acc_s[m])
    start(stage0(0))
    finish2(1)

    def series_back(t, carry):
        rows = aligned(t * TIME_ROWS, TIME_ROWS)
        grad = mm_nt(back_s[0, rows, :], tw_ref[0]) + mm_nt(back_s[1, rows, :], tw_ref[1])
        grad = grad + mm_nt(back_s[2, rows, :], tw_ref[2])
        x = x_s[rows, :].astype(F32)
        t_sg[rows, :] = (t_sg[rows, :].astype(F32) + row_back(x, grad)).astype(BF16)
        return carry

    lax.fori_loop(0, chunks // 4, series_back, 0)
    finish0(0)
    lax.fori_loop(chunks // 4, chunks, series_back, 0)
    finish1(0)
    grad_copy = pltpu.make_async_copy(t_sg, sgrad_hbm, grad_sem)
    grad_copy.start()
    finish3(1, cg_ref)
    finish2(0)
    finish3(0, tg_ref)

    grad_copy.wait()
    out_copy.wait()
    for k in range(parts - 1):
        for seg in range(segments):
            inward(k, seg).wait_send()
        for seg in range(first_late):
            back(k, seg).wait_send()
        for t in range(chunks):
            for n in range(late):
                back_part(k, n, t).wait_send()


SETTLE_PARTS = 2


def settle_kernel(count, *refs):
    sources, results, held = refs[:count], refs[count : 2 * count], refs[2 * count : 3 * count]
    in_sem, out_sem = refs[3 * count :]
    loads, stores = [], []
    for n in range(count):
        step = held[n].shape[0] // SETTLE_PARTS
        for part in range(SETTLE_PARTS):
            rows = pl.ds(part * step, step)
            loads.append(pltpu.make_async_copy(sources[n].at[rows], held[n].at[rows], in_sem.at[n, part]))
            stores.append(pltpu.make_async_copy(held[n].at[rows], results[n].at[rows], out_sem.at[n, part]))
    for load in loads:
        load.start()
    for load, store in zip(loads, stores):
        load.wait()
        store.start()
    for store in stores:
        store.wait()


def settle(*arrays):
    count = len(arrays)
    hbm = pl.BlockSpec(memory_space=pl.ANY)
    return pl.pallas_call(
        functools.partial(settle_kernel, count),
        out_shape=tuple(jax.ShapeDtypeStruct(a.shape, a.dtype) for a in arrays),
        in_specs=[hbm] * count,
        out_specs=(hbm,) * count,
        scratch_shapes=[pltpu.VMEM(a.shape, a.dtype) for a in arrays]
        + [pltpu.SemaphoreType.DMA((count, SETTLE_PARTS))] * 2,
        name="settle",
    )(*arrays)


VMEM_LIMIT = 62 * 1024 * 1024


def shards(series, upstream_grad, time_weights, channel_weights, neighbors):
    parts, dp = lax.axis_size("mp"), lax.axis_size("dp")
    own, length, features = series.shape[1:]
    channels, segments = upstream_grad.shape[1:3]
    blocks_n, near = neighbors.shape
    block = channels // blocks_n
    matrices = time_weights.shape[0]
    total = own * length
    chunks = total // TIME_ROWS
    row_step = min(channels, 512)
    steps = channels // row_step
    slots = 4 if blocks_n <= 4 else 2
    mine = features // parts
    width = features * matrices // dp
    tiles = features // GROUP
    upstream = jnp.swapaxes(upstream_grad.reshape(channels, segments, tiles, GROUP), 1, 2)
    vmem = pl.BlockSpec(memory_space=pltpu.VMEM)
    hbm = pl.BlockSpec(memory_space=pl.ANY)
    dma = lambda *shape: pltpu.SemaphoreType.DMA(shape)
    b16 = lambda *shape: pltpu.VMEM(shape, BF16)
    f32 = lambda *shape: pltpu.VMEM(shape, F32)
    grads = jax.ShapeDtypeStruct((matrices, mine, features), F32)
    per_block = (blocks_n, block, features)
    contributions = f32(blocks_n * near + 1, block, features)
    output, series_grad, time_grads, channel_grads = pl.pallas_call(
        functools.partial(layer_kernel, parts, dp, length),
        out_shape=(
            jax.ShapeDtypeStruct((channels * segments * tiles, GROUP), BF16),
            jax.ShapeDtypeStruct((total, features), BF16),
            grads,
            grads,
        ),
        in_specs=[pl.BlockSpec(memory_space=pltpu.SMEM), hbm, hbm, hbm, hbm],
        out_specs=(hbm, hbm, vmem, vmem),
        scratch_shapes=[
            b16(*time_weights.shape),
            b16(*channel_weights.shape),
            b16(total, features),
            b16(channels * segments * tiles, GROUP),
            b16(segments, channels, features),
            b16(length, own, features),
            b16(segments, channels, features),
            b16(segments, channels, features),
            b16(length, own, features),
            b16(chunks, features, TIME_ROWS),
            b16(total, features),
            b16(total, features),
            b16(chunks, features, TIME_ROWS),
            b16(total, features),
            f32(total, features),
            f32(total, features),
            b16(total // GROUP, GROUP, HEADS * GROUP),
            b16(chunks, features, TIME_ROWS),
            b16(total, features),
            b16(3, total, features),
            b16(*per_block),
            b16(*per_block),
            b16(*per_block),
            b16(*per_block),
            b16(blocks_n, features, block),
            b16(blocks_n, features, block),
            f32(*per_block),
            f32(*per_block),
            b16(*per_block),
            contributions,
            contributions,
            b16(segments, channels, features),
            b16(segments, blocks_n, features, block),
            b16(segments, steps, features, row_step),
            b16(slots, HEADS * GROUP, features),
            b16(slots, HEADS * GROUP, features),
            f32(GROUP, GROUP),
            f32(matrices, features, features),
            b16(2, 2, dp // 2, features, width),
            b16(2, dp // 2, features, width),
            b16(2, dp // 2, features, width),
            b16(2, dp // 2 - 1, features, width),
            b16(2, parts, mine, width),
            b16(2, parts - 1, mine, width),
            b16(2, mine, width),
            b16(2, dp, mine, width),
            dma(2), dma(chunks), pltpu.SemaphoreType.DMA, pltpu.SemaphoreType.DMA, pltpu.SemaphoreType.DMA,
            dma(parts - 1, segments), dma(parts - 1, segments),
            dma(parts - 1, segments), dma(parts - 1, segments),
            dma(parts - 1, min(2, segments), chunks), dma(parts - 1, min(2, segments), chunks),
            dma(2), dma(2), dma(2, dp // 2 - 1), dma(2, dp // 2 - 1), dma(2, parts - 1), dma(2, parts - 1), dma(2, dp - 1), dma(2, dp - 1),
        ],
        compiler_params=pltpu.CompilerParams(
            vmem_limit_bytes=VMEM_LIMIT, collective_id=0, has_side_effects=True
        ),
        name="layer",
    )(
        neighbors,
        series.reshape(total, features),
        upstream.reshape(channels * segments * tiles, GROUP),
        time_weights,
        channel_weights,
    )
    output, series_grad, time_grads, channel_grads = settle(output, series_grad, time_grads, channel_grads)
    output = jnp.swapaxes(output.reshape(channels, tiles, segments, GROUP), 1, 2)
    return (
        output.reshape(upstream_grad.shape),
        series_grad.reshape(series.shape),
        time_grads,
        channel_grads,
    )


def solution(mesh):
    placed = (P("dp", "mp", None, None), P("dp", None, "mp", None), P(), P(), P())
    return jax.shard_map(
        shards,
        mesh=mesh,
        in_specs=placed,
        out_specs=(
            P("dp", None, "mp", None),
            P("dp", "mp", None, None),
            P(None, "mp", None),
            P(None, "mp", None),
        ),
        check_vma=False,
    )
```

```python
import functools

import jax
import jax.numpy as jnp
from jax import lax
from jax.experimental import pallas as pl
from jax.experimental.pallas import tpu as pltpu
from jax.sharding import PartitionSpec as P

HEADS = 4
EPS = 1e-06
LOGIT_SCALE = 0.25
EXP2_SCALE = LOGIT_SCALE * 1.4426950408889634
GROUP = 128
TIME_ROWS = 512
PERM_ROWS = 256

F32 = jnp.float32
BF16 = jnp.bfloat16
MESH = pl.DeviceIdType.MESH


def mm(a, b):
    return lax.dot_general(a, b, (((1,), (0,)), ((), ())), preferred_element_type=F32)


def mm_nt(a, b):
    return lax.dot_general(a, b, (((1,), (1,)), ((), ())), preferred_element_type=F32)


def iota(shape, dim):
    return lax.broadcasted_iota(jnp.int32, shape, dim)


def eye(size):
    return jnp.where(iota((size, size), 0) == iota((size, size), 1), 1.0, 0.0).astype(BF16)


def regroup(outer, inner):
    size = outer * inner
    row, col = iota((size, size), 0), iota((size, size), 1)
    source = lax.rem(row, outer) * inner + row // outer
    return jnp.where(col == source, 1.0, 0.0).astype(BF16)


def head_blocks(features):
    width = features // HEADS
    rows = iota((features, features), 0) // width
    cols = iota((features, features), 1) // width
    return jnp.where(rows == cols, 1.0 / width, 0.0).astype(BF16)


def inv_rms(values):
    return lax.rsqrt(jnp.mean(values * values, axis=-1, keepdims=True) + EPS)


def head_hat(raw, blocks):
    inv = lax.rsqrt(mm((raw * raw).astype(BF16), blocks) + EPS)
    return (raw * inv).astype(BF16), inv


def head_back(hat_b, inv, grad, blocks):
    hat = hat_b.astype(F32)
    return (inv * (grad - hat * mm((hat * grad).astype(BF16), blocks))).astype(BF16)


def row_back(rows, grad):
    inv = inv_rms(rows)
    hat = rows * inv
    return inv * (grad - hat * jnp.mean(hat * grad, axis=-1, keepdims=True))


def fill_heads(ref, rows):
    width = rows.shape[1] // HEADS
    per_tile = GROUP // width
    tile_head = iota((GROUP, GROUP), 1) // width
    for h in range(HEADS):
        lanes = slice((h // per_tile) * GROUP, (h // per_tile + 1) * GROUP)
        keep = jnp.where(tile_head == h % per_tile, 1.0, 0.0).astype(BF16)
        ref[h * GROUP : (h + 1) * GROUP, lanes] = rows[:, lanes] * keep


def head_product(features_by_keys, keys_by_queries):
    features = features_by_keys.shape[0]
    width = features // HEADS
    per_tile = GROUP // width
    parts = []
    for tile in range(features // GROUP):
        cols = slice(tile * per_tile * GROUP, (tile + 1) * per_tile * GROUP)
        both = mm(features_by_keys[tile * GROUP : (tile + 1) * GROUP, :], keys_by_queries[:, cols])
        for h in range(per_tile):
            parts.append(both[h * width : (h + 1) * width, h * GROUP : (h + 1) * GROUP])
    return jnp.concatenate(parts, axis=0)


def others(axis, size):
    me = lax.axis_index(axis)
    return [lax.rem(me + k, size) for k in range(1, size)]


def aligned(start, size):
    return pl.ds(pl.multiple_of(start, size), size)


def layer_kernel(
    parts, dp, length,
    nb_ref, x_hbm, up_hbm, tw_hbm, cw_hbm,
    out_hbm, sgrad_hbm, tg_ref, cg_ref,
    tw_ref, cw_ref, x_s, up_raw, up_s, stream_s, cols_s, sg_s, ret_s,
    t_nT, t_q, t_k, t_kT, t_v, t_iq, t_ik, t_w, t_mT, t_sg, back_s,
    c_q, c_k, c_v, c_g, c_kT, c_vT, c_iq, c_ik, c_dq, c_dk, c_dv, c_m, c_mT, c_nT,
    qbd, gbd, tile_keep, acc_s, all_s, core_in, chip_s, dp_in, mp_mine, mp_in, done_s, done_in,
    w_sem, x_sem, up_sem, out_sem, grad_sem, in_send, in_recv, back_send, back_recv, last_send, last_recv,
    send0, recv0, send1, recv1, send2, recv2, send3, recv3,
):
    segments, channels, features = up_s.shape
    own = stream_s.shape[1]
    rows_total = x_s.shape[0]
    chunks = rows_total // TIME_ROWS
    per_chunk = TIME_ROWS // length
    groups = TIME_ROWS // GROUP
    blocks_n, near = nb_ref.shape
    block = channels // blocks_n
    slots = qbd.shape[0]
    me = lax.axis_index("mp")
    me_dp = lax.axis_index("dp")
    peers = others("mp", parts)
    if parts == 4:
        peers = [lax.rem(me + 2, 4), 3 - me, me + 1 - 2 * lax.rem(me, 2)]
    dp_peers = others("dp", dp)

    def load_x(t):
        return pltpu.make_async_copy(
            x_hbm.at[aligned(t * TIME_ROWS, TIME_ROWS)], x_s.at[aligned(t * TIME_ROWS, TIME_ROWS)], x_sem.at[t]
        )

    def load_up():
        return pltpu.make_async_copy(up_hbm, up_raw, up_sem)

    load_weights = [
        pltpu.make_async_copy(tw_hbm, tw_ref, w_sem.at[0]),
        pltpu.make_async_copy(cw_hbm, cw_ref, w_sem.at[1]),
    ]
    load_x(0).start()
    load_weights[0].start()
    for t in range(1, chunks):
        load_x(t).start()
    load_weights[1].start()
    load_up().start()

    barrier = pltpu.get_barrier_semaphore()
    for peer in peers:
        pl.semaphore_signal(barrier, inc=1, device_id={"mp": peer}, device_id_type=MESH)
    for peer in dp_peers:
        pl.semaphore_signal(barrier, inc=1, device_id={"dp": peer}, device_id_type=MESH)

    blocks = head_blocks(features)
    cg = PERM_ROWS // length
    perm_t = regroup(cg, length)
    perm_tb = regroup(length, cg)
    tiles = features // GROUP
    sg_group = PERM_ROWS // (tiles * segments)
    qbd[...] = jnp.zeros_like(qbd)
    gbd[...] = jnp.zeros_like(gbd)
    tile_keep[...] = jnp.where(
        iota((GROUP, GROUP), 0) // length == iota((GROUP, GROUP), 1) // length, 1.0, 0.0
    ).astype(F32)
    c_dk[blocks_n * near] = jnp.zeros((block, features), F32)
    c_dv[blocks_n * near] = jnp.zeros((block, features), F32)

    load_weights[0].wait()

    def inward(k, seg):
        return pltpu.make_async_remote_copy(
            src_ref=stream_s.at[peers[k] * segments + seg],
            dst_ref=cols_s.at[seg, aligned(me * own, own)],
            send_sem=in_send.at[k, seg],
            recv_sem=in_recv.at[k, seg],
            device_id={"mp": peers[k]},
            device_id_type=MESH,
        )

    def inward_part(k, seg, t):
        return pltpu.make_async_remote_copy(
            src_ref=stream_s.at[peers[k] * segments + seg, aligned(t * per_chunk, per_chunk)],
            dst_ref=cols_s.at[seg, aligned(me * own + t * per_chunk, per_chunk)],
            send_sem=in_send.at[k, seg],
            recv_sem=in_recv.at[k, seg],
            device_id={"mp": peers[k]},
            device_id_type=MESH,
        )

    def back(k, seg):
        return pltpu.make_async_remote_copy(
            src_ref=sg_s.at[seg, aligned(peers[k] * own, own)],
            dst_ref=ret_s.at[me * segments + seg],
            send_sem=back_send.at[k, seg],
            recv_sem=back_recv.at[k, seg],
            device_id={"mp": peers[k]},
            device_id_type=MESH,
        )

    late = min(2, segments)
    first_late = segments - late

    def back_part(k, n, t):
        seg = first_late + n
        return pltpu.make_async_remote_copy(
            src_ref=sg_s.at[seg, aligned(peers[k] * own + t * per_chunk, per_chunk)],
            dst_ref=ret_s.at[me * segments + seg, aligned(t * per_chunk, per_chunk)],
            send_sem=last_send.at[k, n, t],
            recv_sem=last_recv.at[k, n, t],
            device_id={"mp": peers[k]},
            device_id_type=MESH,
        )

    def time_forward(t, carry):
        load_x(t).wait()
        rows = aligned(t * TIME_ROWS, TIME_ROWS)
        x = x_s[rows, :].astype(F32)
        normed = (x * inv_rms(x)).astype(BF16)
        t_nT[t] = normed.T
        q, iq = head_hat(mm(normed, tw_ref[0]), blocks)
        k, ik = head_hat(mm(normed, tw_ref[1]), blocks)
        v = mm(normed, tw_ref[2]).astype(BF16)
        t_q[rows, :], t_k[rows, :], t_v[rows, :] = q, k, v
        t_iq[rows, :], t_ik[rows, :] = iq, ik
        t_kT[t] = k.T
        vT = v.T
        keep = jnp.concatenate([tile_keep[...]] * HEADS, axis=1)
        mixed = []
        for g in range(groups):
            sl = slice(g * GROUP, (g + 1) * GROUP)
            bd = qbd.at[g % slots]
            fill_heads(bd, q[sl])
            e = jnp.exp2(EXP2_SCALE * mm_nt(k[sl], bd[...])) * keep
            w = (e * (1.0 / jnp.sum(e, axis=0, keepdims=True))).astype(BF16)
            t_w[t * groups + g] = w
            mT = head_product(vT[:, sl], w).astype(BF16)
            t_mT[t, :, sl] = mT
            mixed.append(mT.T)
        stream = (x + mm(jnp.concatenate(mixed, axis=0), tw_ref[3])).astype(BF16)
        for part in range(TIME_ROWS // PERM_ROWS):
            ordered = mm(perm_t, stream[part * PERM_ROWS : (part + 1) * PERM_ROWS]).astype(BF16)
            for seg in range(length):
                stream_s[seg, aligned(t * per_chunk + part * cg, cg), :] = ordered[seg * cg : (seg + 1) * cg]
        @pl.when(t == 0)
        def _():
            pl.semaphore_wait(barrier, len(peers) + len(dp_peers))

        for peer in range(parts - 1):
            inward_part(peer, 0, t).start()
        if segments > 1:

            @pl.when(t < chunks // 2)
            def _():
                for peer in range(parts - 1):
                    inward_part(peer, 1, t).start()

        return carry

    lax.fori_loop(0, chunks, time_forward, 0)
    for seg in range(1, segments):
        for k in range(parts - 1):
            if seg == 1:
                for t in range(chunks // 2, chunks):
                    inward_part(k, seg, t).start()
            else:
                inward(k, seg).start()
    for seg in range(segments):
        cols_s[seg, aligned(me * own, own), :] = stream_s[me * segments + seg]

    load_up().wait()
    load_weights[1].wait()
    perm_u = regroup(sg_group, tiles * segments)
    perm_ub = regroup(tiles * segments, sg_group)

    def order_up(pair, carry):
        both = [up_raw[aligned((pair * 2 + n) * PERM_ROWS, PERM_ROWS), :] for n in range(2)]
        ordered = mm(perm_u, jnp.concatenate(both, axis=1)).astype(BF16)
        for n in range(2):
            for tile in range(tiles):
                for seg in range(segments):
                    at = (tile * segments + seg) * sg_group
                    up_s[seg, aligned((pair * 2 + n) * sg_group, sg_group), tile * GROUP : (tile + 1) * GROUP] = ordered[
                        at : at + sg_group, n * GROUP : (n + 1) * GROUP
                    ]
        return carry

    lax.fori_loop(0, channels // (2 * sg_group), order_up, 0, unroll=True)

    row_step = min(channels, 512)
    step_blocks = row_step // block

    def one_segment(seg, carry):
        for k in range(parts - 1):
            inward(k, seg).wait_recv()

        def project(r, inner):
            rows = aligned(r * row_step, row_step)
            these = pl.ds(r * step_blocks, step_blocks)
            x = cols_s[seg, rows, :].astype(F32)
            normed = (x * inv_rms(x)).astype(BF16)
            c_nT[seg, r] = normed.T
            q, iq = head_hat(mm(normed, cw_ref[0]), blocks)
            k, ik = head_hat(mm(normed, cw_ref[1]), blocks)
            v = mm(normed, cw_ref[2]).astype(BF16)
            shaped = (step_blocks, block, features)
            c_q[these], c_k[these], c_v[these] = q.reshape(shaped), k.reshape(shaped), v.reshape(shaped)
            c_iq[these], c_ik[these] = iq.reshape(shaped), ik.reshape(shaped)
            kT = k.T
            vT = v.T
            for b in range(step_blocks):
                c_kT[r * step_blocks + b] = kT[:, b * block : (b + 1) * block]
                c_vT[r * step_blocks + b] = vT[:, b * block : (b + 1) * block]
            c_g[these] = mm_nt(up_s[seg, rows, :], cw_ref[3]).astype(BF16).reshape(shaped)
            return inner

        lax.fori_loop(0, channels // row_step, project, 0)

        def attend(pair, inner):
            for slot in range(slots):
                i = pair * slots + slot
                ids = [nb_ref[i, n] for n in range(near)]
                bd, gd = qbd.at[slot], gbd.at[slot]
                fill_heads(bd, c_q[i])
                fill_heads(gd, c_g[i])
                k_near = jnp.concatenate([c_k[j] for j in ids], axis=0)
                v_near = jnp.concatenate([c_v[j] for j in ids], axis=0)
                kT_near = jnp.concatenate([c_kT[j] for j in ids], axis=1)
                vT_near = jnp.concatenate([c_vT[j] for j in ids], axis=1)
                e = jnp.exp2(EXP2_SCALE * mm_nt(k_near, bd[...]))
                w = e * (1.0 / jnp.sum(e, axis=0, keepdims=True))
                w_b = w.astype(BF16)
                grad = mm_nt(v_near, gd[...])
                delta = jnp.sum(w * grad, axis=0, keepdims=True)
                t_b = (w * (grad - delta)).astype(BF16)
                mT = head_product(vT_near, w_b).astype(BF16)
                c_mT[seg, i] = mT
                c_m[seg, aligned(i * block, block), :] = mT.T
                dqT = (LOGIT_SCALE * head_product(kT_near, t_b)).astype(BF16)
                c_dq[i] = dqT.T
                c_dk[pl.ds(i * near, near)] = mm(t_b, bd[...]).reshape(near, block, features)
                c_dv[pl.ds(i * near, near)] = mm(w_b, gd[...]).reshape(near, block, features)
            return inner

        lax.fori_loop(0, blocks_n // slots, attend, 0)

        def finish_block(j):
            def place(i):
                at = blocks_n * near
                for n in range(1, near):
                    at = jnp.where(nb_ref[i, n] == j, i * near + n, at)
                return at

            def more(m, sums):
                at = place(lax.rem(j + m, blocks_n))
                return sums[0] + c_dk[at], sums[1] + c_dv[at]

            sums = (c_dk[j * near], c_dv[j * near])
            if blocks_n <= 4:
                for m in range(1, blocks_n):
                    sums = more(m, sums)
            else:
                sums = lax.fori_loop(1, blocks_n, more, sums)
            rows = aligned(j * block, block)
            qb = head_back(c_q[j], c_iq[j], c_dq[j].astype(F32), blocks)
            kb = head_back(c_k[j], c_ik[j], LOGIT_SCALE * sums[0], blocks)
            vb = sums[1].astype(BF16)
            at_rows = aligned(seg * channels + j * block, block)
            back_s[0, at_rows, :] = qb
            back_s[1, at_rows, :] = kb
            back_s[2, at_rows, :] = vb
            grad = mm_nt(qb, cw_ref[0]) + mm_nt(kb, cw_ref[1]) + mm_nt(vb, cw_ref[2])
            x = cols_s[seg, rows, :].astype(F32)
            sg_s[seg, rows, :] = (up_s[seg, rows, :].astype(F32) + row_back(x, grad)).astype(BF16)

        def finish(group, inner):
            for n in range(slots):
                finish_block(group * slots + n)
            return inner

        lax.fori_loop(0, blocks_n // slots, finish, 0)

        @pl.when(seg < first_late)
        def _():
            for k in range(parts - 1):
                back(k, seg).start()

        if late > 1:

            @pl.when(seg == first_late)
            def _():
                for t in range(chunks // 4):
                    for k in range(parts - 1):
                        back_part(k, 0, t).start()

        ret_s[me * segments + seg] = sg_s[seg, aligned(me * own, own), :]
        return carry

    lax.fori_loop(0, segments, one_segment, 0)
    for t in range(chunks):
        for n in range(late):
            if n < late - 1 and t < chunks // 4:
                continue
            for k in range(parts - 1):
                back_part(k, n, t).start()

    matrices = tw_ref.shape[0]
    width = all_s.shape[4]
    core, chip = lax.rem(me_dp, 2), me_dp // 2
    chips = dp // 2
    chip_peers = [lax.rem(chip + k, chips) for k in range(1, chips)]
    splits = features // width

    def exchange(src, dst, send, recv, device):
        return pltpu.make_async_remote_copy(
            src_ref=src, dst_ref=dst, send_sem=send, recv_sem=recv, device_id=device, device_id_type=MESH
        )

    def put_grad(r, m, value):
        for part in range(splits):
            place = m * splits + part
            all_s[r, place % 2, place // 2] = value[:, part * width : (part + 1) * width].astype(BF16)

    def stage0(r):
        return [exchange(all_s.at[r, 1 - core], core_in.at[r], send0.at[r], recv0.at[r], {"dp": me_dp + 1 - 2 * core})]

    def stage1(r):
        return [
            exchange(chip_s.at[r, p], dp_in.at[r, k], send1.at[r, k], recv1.at[r, k], {"dp": p * 2 + core})
            for k, p in enumerate(chip_peers)
        ]

    def stage2(r):
        return [
            exchange(mp_mine.at[r, p], mp_in.at[r, k], send2.at[r, k], recv2.at[r, k], {"mp": p})
            for k, p in enumerate(peers)
        ]

    def stage3(r):
        return [
            exchange(done_s.at[r], done_in.at[r, me_dp], send3.at[r, k], recv3.at[r, k], {"dp": p})
            for k, p in enumerate(dp_peers)
        ]

    def start(copies):
        for copy in copies:
            copy.start()

    def wait(copies):
        for copy in copies:
            copy.wait()

    def finish0(r):
        wait(stage0(r))
        chip_s[r] = (all_s[r, core].astype(F32) + core_in[r].astype(F32)).astype(BF16)
        start(stage1(r))

    def finish1(r):
        wait(stage1(r))
        total = chip_s[r, chip].astype(F32)
        for k in range(chips - 1):
            total = total + dp_in[r, k].astype(F32)
        mp_mine[r] = total.astype(BF16).reshape(mp_mine.shape[1:])
        start(stage2(r))

    def finish2(r):
        wait(stage2(r))
        total = mp_mine[r, me].astype(F32)
        for k in range(parts - 1):
            total = total + mp_in[r, k].astype(F32)
        done_s[r] = total.astype(BF16)
        start(stage3(r))
        done_in[r, me_dp] = done_s[r]

    def finish3(r, ref):
        wait(stage3(r))
        for m in range(matrices):
            for part in range(splits):
                ref[m, :, part * width : (part + 1) * width] = done_in[r, m * splits + part].astype(F32) / dp

    steps = channels // row_step
    for m in range(matrices):
        total = None
        for seg in range(segments):
            for r in range(steps):
                rows = slice(r * row_step, (r + 1) * row_step)
                if m < 3:
                    term = mm(c_nT[seg, r], back_s[m, seg * channels + r * row_step : seg * channels + (r + 1) * row_step, :])
                else:
                    mT = jnp.concatenate([c_mT[seg, r * step_blocks + b] for b in range(step_blocks)], axis=1)
                    term = mm(mT, up_s[seg, rows, :])
                total = term if total is None else total + term
        put_grad(1, m, total)
    start(stage0(1))


    def project_out(r, carry):
        rows = aligned(r * row_step, row_step)
        for seg in range(segments):
            res = cols_s[seg, rows, :].astype(F32) + mm(c_m[seg, rows, :], cw_ref[3])
            c_m[seg, rows, :] = res.astype(BF16)
        return carry

    def order_out(pair, carry):
        both = []
        for n in range(2):
            rows = aligned((pair * 2 + n) * sg_group, sg_group)
            both.append(
                jnp.concatenate(
                    [
                        c_m[seg, rows, tile * GROUP : (tile + 1) * GROUP]
                        for tile in range(tiles)
                        for seg in range(segments)
                    ],
                    axis=0,
                )
            )
        ordered = mm(perm_ub, jnp.concatenate(both, axis=1)).astype(BF16)
        for n in range(2):
            up_raw[aligned((pair * 2 + n) * PERM_ROWS, PERM_ROWS), :] = ordered[:, n * GROUP : (n + 1) * GROUP]
        return carry

    out_copy = pltpu.make_async_copy(up_raw, out_hbm, out_sem)

    lax.fori_loop(0, channels // row_step, project_out, 0)
    lax.fori_loop(0, channels // (2 * sg_group), order_out, 0, unroll=True)
    out_copy.start()
    finish0(1)
    for seg in range(first_late):
        for k in range(parts - 1):
            back(k, seg).wait_recv()

    def time_backward(t, carry):
        for n in range(late):
            for k in range(parts - 1):
                back_part(k, n, t).wait_recv()
        rows = aligned(t * TIME_ROWS, TIME_ROWS)
        ordered = []
        for part in range(TIME_ROWS // PERM_ROWS):
            at = aligned(t * per_chunk + part * cg, cg)
            slabs = jnp.concatenate([ret_s[seg, at, :] for seg in range(length)], axis=0)
            ordered.append(mm(perm_tb, slabs).astype(BF16))
        up_b = jnp.concatenate(ordered, axis=0)
        t_sg[rows, :] = up_b
        mg = mm_nt(up_b, tw_ref[3]).astype(BF16)
        q, k, v = t_q[rows, :], t_k[rows, :], t_v[rows, :]
        kT = t_kT[t]
        dq, dk, dv = [], [], []
        for g in range(groups):
            sl = slice(g * GROUP, (g + 1) * GROUP)
            bd, gd = qbd.at[g % slots], gbd.at[g % slots]
            fill_heads(bd, q[sl])
            fill_heads(gd, mg[sl])
            w_b = t_w[t * groups + g]
            w = w_b.astype(F32)
            grad = mm_nt(v[sl], gd[...])
            delta = jnp.sum(w * grad, axis=0, keepdims=True)
            t_b = (w * (grad - delta)).astype(BF16)
            dqT = (LOGIT_SCALE * head_product(kT[:, sl], t_b)).astype(BF16)
            dq.append(dqT.T.astype(F32))
            dk.append(LOGIT_SCALE * mm(t_b, bd[...]))
            dv.append(mm(w_b, gd[...]).astype(BF16))
        qb = head_back(q, t_iq[rows, :], jnp.concatenate(dq, axis=0), blocks)
        kb = head_back(k, t_ik[rows, :], jnp.concatenate(dk, axis=0), blocks)
        vb = jnp.concatenate(dv, axis=0)
        back_s[0, rows, :] = qb
        back_s[1, rows, :] = kb
        back_s[2, rows, :] = vb
        nT = t_nT[t]
        first = t == 0
        for m, back_rows in enumerate((qb, kb, vb)):
            acc_s[m] = mm(nT, back_rows) + jnp.where(first, 0.0, acc_s[m])
        acc_s[3] = mm(t_mT[t], up_b) + jnp.where(first, 0.0, acc_s[3])
        pl.when(t == 0)(functools.partial(finish1, 1))
        return carry

    acc_s[...] = jnp.zeros_like(acc_s)
    lax.fori_loop(0, chunks, time_backward, 0)
    for m in range(matrices):
        put_grad(0, m, acc_s[m])
    start(stage0(0))

    def series_back(t, carry):
        rows = aligned(t * TIME_ROWS, TIME_ROWS)
        grad = mm_nt(back_s[0, rows, :], tw_ref[0]) + mm_nt(back_s[1, rows, :], tw_ref[1])
        grad = grad + mm_nt(back_s[2, rows, :], tw_ref[2])
        x = x_s[rows, :].astype(F32)
        t_sg[rows, :] = (t_sg[rows, :].astype(F32) + row_back(x, grad)).astype(BF16)
        return carry

    lax.fori_loop(0, chunks // 4, series_back, 0)
    finish0(0)
    finish2(1)
    lax.fori_loop(chunks // 4, chunks, series_back, 0)
    finish1(0)
    grad_copy = pltpu.make_async_copy(t_sg, sgrad_hbm, grad_sem)
    grad_copy.start()
    finish3(1, cg_ref)
    finish2(0)
    finish3(0, tg_ref)

    grad_copy.wait()
    out_copy.wait()
    for k in range(parts - 1):
        for seg in range(segments):
            inward(k, seg).wait_send()
        for seg in range(first_late):
            back(k, seg).wait_send()
        for t in range(chunks):
            for n in range(late):
                back_part(k, n, t).wait_send()


SETTLE_PARTS = 2


def settle_kernel(count, *refs):
    sources, results, held = refs[:count], refs[count : 2 * count], refs[2 * count : 3 * count]
    in_sem, out_sem = refs[3 * count :]
    loads, stores = [], []
    for n in range(count):
        step = held[n].shape[0] // SETTLE_PARTS
        for part in range(SETTLE_PARTS):
            rows = pl.ds(part * step, step)
            loads.append(pltpu.make_async_copy(sources[n].at[rows], held[n].at[rows], in_sem.at[n, part]))
            stores.append(pltpu.make_async_copy(held[n].at[rows], results[n].at[rows], out_sem.at[n, part]))
    for load in loads:
        load.start()
    for load, store in zip(loads, stores):
        load.wait()
        store.start()
    for store in stores:
        store.wait()


def settle(*arrays):
    count = len(arrays)
    hbm = pl.BlockSpec(memory_space=pl.ANY)
    return pl.pallas_call(
        functools.partial(settle_kernel, count),
        out_shape=tuple(jax.ShapeDtypeStruct(a.shape, a.dtype) for a in arrays),
        in_specs=[hbm] * count,
        out_specs=(hbm,) * count,
        scratch_shapes=[pltpu.VMEM(a.shape, a.dtype) for a in arrays]
        + [pltpu.SemaphoreType.DMA((count, SETTLE_PARTS))] * 2,
        name="settle",
    )(*arrays)


VMEM_LIMIT = 62 * 1024 * 1024


def shards(series, upstream_grad, time_weights, channel_weights, neighbors):
    parts, dp = lax.axis_size("mp"), lax.axis_size("dp")
    own, length, features = series.shape[1:]
    channels, segments = upstream_grad.shape[1:3]
    blocks_n, near = neighbors.shape
    block = channels // blocks_n
    matrices = time_weights.shape[0]
    total = own * length
    chunks = total // TIME_ROWS
    row_step = min(channels, 512)
    steps = channels // row_step
    slots = 4 if blocks_n <= 4 else 2
    mine = features // parts
    width = features * matrices // dp
    tiles = features // GROUP
    upstream = jnp.swapaxes(upstream_grad.reshape(channels, segments, tiles, GROUP), 1, 2)
    vmem = pl.BlockSpec(memory_space=pltpu.VMEM)
    hbm = pl.BlockSpec(memory_space=pl.ANY)
    dma = lambda *shape: pltpu.SemaphoreType.DMA(shape)
    b16 = lambda *shape: pltpu.VMEM(shape, BF16)
    f32 = lambda *shape: pltpu.VMEM(shape, F32)
    grads = jax.ShapeDtypeStruct((matrices, mine, features), F32)
    per_block = (blocks_n, block, features)
    contributions = f32(blocks_n * near + 1, block, features)
    output, series_grad, time_grads, channel_grads = pl.pallas_call(
        functools.partial(layer_kernel, parts, dp, length),
        out_shape=(
            jax.ShapeDtypeStruct((channels * segments * tiles, GROUP), BF16),
            jax.ShapeDtypeStruct((total, features), BF16),
            grads,
            grads,
        ),
        in_specs=[pl.BlockSpec(memory_space=pltpu.SMEM), hbm, hbm, hbm, hbm],
        out_specs=(hbm, hbm, vmem, vmem),
        scratch_shapes=[
            b16(*time_weights.shape),
            b16(*channel_weights.shape),
            b16(total, features),
            b16(channels * segments * tiles, GROUP),
            b16(segments, channels, features),
            b16(length, own, features),
            b16(segments, channels, features),
            b16(segments, channels, features),
            b16(length, own, features),
            b16(chunks, features, TIME_ROWS),
            b16(total, features),
            b16(total, features),
            b16(chunks, features, TIME_ROWS),
            b16(total, features),
            f32(total, features),
            f32(total, features),
            b16(total // GROUP, GROUP, HEADS * GROUP),
            b16(chunks, features, TIME_ROWS),
            b16(total, features),
            b16(3, total, features),
            b16(*per_block),
            b16(*per_block),
            b16(*per_block),
            b16(*per_block),
            b16(blocks_n, features, block),
            b16(blocks_n, features, block),
            f32(*per_block),
            f32(*per_block),
            b16(*per_block),
            contributions,
            contributions,
            b16(segments, channels, features),
            b16(segments, blocks_n, features, block),
            b16(segments, steps, features, row_step),
            b16(slots, HEADS * GROUP, features),
            b16(slots, HEADS * GROUP, features),
            f32(GROUP, GROUP),
            f32(matrices, features, features),
            b16(2, 2, dp // 2, features, width),
            b16(2, dp // 2, features, width),
            b16(2, dp // 2, features, width),
            b16(2, dp // 2 - 1, features, width),
            b16(2, parts, mine, width),
            b16(2, parts - 1, mine, width),
            b16(2, mine, width),
            b16(2, dp, mine, width),
            dma(2), dma(chunks), pltpu.SemaphoreType.DMA, pltpu.SemaphoreType.DMA, pltpu.SemaphoreType.DMA,
            dma(parts - 1, segments), dma(parts - 1, segments),
            dma(parts - 1, segments), dma(parts - 1, segments),
            dma(parts - 1, min(2, segments), chunks), dma(parts - 1, min(2, segments), chunks),
            dma(2), dma(2), dma(2, dp // 2 - 1), dma(2, dp // 2 - 1), dma(2, parts - 1), dma(2, parts - 1), dma(2, dp - 1), dma(2, dp - 1),
        ],
        compiler_params=pltpu.CompilerParams(
            vmem_limit_bytes=VMEM_LIMIT, collective_id=0, has_side_effects=True
        ),
        name="layer",
    )(
        neighbors,
        series.reshape(total, features),
        upstream.reshape(channels * segments * tiles, GROUP),
        time_weights,
        channel_weights,
    )
    output, series_grad, time_grads, channel_grads = settle(output, series_grad, time_grads, channel_grads)
    output = jnp.swapaxes(output.reshape(channels, tiles, segments, GROUP), 1, 2)
    return (
        output.reshape(upstream_grad.shape),
        series_grad.reshape(series.shape),
        time_grads,
        channel_grads,
    )


def solution(mesh):
    placed = (P("dp", "mp", None, None), P("dp", None, "mp", None), P(), P(), P())
    return jax.shard_map(
        shards,
        mesh=mesh,
        in_specs=placed,
        out_specs=(
            P("dp", None, "mp", None),
            P("dp", "mp", None, None),
            P(None, "mp", None),
            P(None, "mp", None),
        ),
        check_vma=False,
    )
```

```python
import functools

import jax
import jax.numpy as jnp
from jax import lax
from jax.experimental import pallas as pl
from jax.experimental.pallas import tpu as pltpu
from jax.sharding import PartitionSpec as P

HEADS = 4
EPS = 1e-06
LOGIT_SCALE = 0.25
EXP2_SCALE = LOGIT_SCALE * 1.4426950408889634
GROUP = 128
TIME_ROWS = 512
PERM_ROWS = 256

F32 = jnp.float32
BF16 = jnp.bfloat16
MESH = pl.DeviceIdType.MESH


def mm(a, b):
    return lax.dot_general(a, b, (((1,), (0,)), ((), ())), preferred_element_type=F32)


def mm_nt(a, b):
    return lax.dot_general(a, b, (((1,), (1,)), ((), ())), preferred_element_type=F32)


def iota(shape, dim):
    return lax.broadcasted_iota(jnp.int32, shape, dim)


def eye(size):
    return jnp.where(iota((size, size), 0) == iota((size, size), 1), 1.0, 0.0).astype(BF16)


def regroup(outer, inner):
    size = outer * inner
    row, col = iota((size, size), 0), iota((size, size), 1)
    source = lax.rem(row, outer) * inner + row // outer
    return jnp.where(col == source, 1.0, 0.0).astype(BF16)


def head_blocks(features):
    width = features // HEADS
    rows = iota((features, features), 0) // width
    cols = iota((features, features), 1) // width
    return jnp.where(rows == cols, 1.0 / width, 0.0).astype(BF16)


def inv_rms(values):
    return lax.rsqrt(jnp.mean(values * values, axis=-1, keepdims=True) + EPS)


def head_hat(raw, blocks):
    inv = lax.rsqrt(mm((raw * raw).astype(BF16), blocks) + EPS)
    return (raw * inv).astype(BF16), inv


def head_back(hat_b, inv, grad, blocks):
    hat = hat_b.astype(F32)
    return (inv * (grad - hat * mm((hat * grad).astype(BF16), blocks))).astype(BF16)


def row_back(rows, grad):
    inv = inv_rms(rows)
    hat = rows * inv
    return inv * (grad - hat * jnp.mean(hat * grad, axis=-1, keepdims=True))


def fill_heads(ref, rows):
    width = rows.shape[1] // HEADS
    per_tile = GROUP // width
    tile_head = iota((GROUP, GROUP), 1) // width
    for h in range(HEADS):
        lanes = slice((h // per_tile) * GROUP, (h // per_tile + 1) * GROUP)
        keep = jnp.where(tile_head == h % per_tile, 1.0, 0.0).astype(BF16)
        ref[h * GROUP : (h + 1) * GROUP, lanes] = rows[:, lanes] * keep


def head_product(features_by_keys, keys_by_queries):
    features = features_by_keys.shape[0]
    width = features // HEADS
    per_tile = GROUP // width
    parts = []
    for tile in range(features // GROUP):
        cols = slice(tile * per_tile * GROUP, (tile + 1) * per_tile * GROUP)
        both = mm(features_by_keys[tile * GROUP : (tile + 1) * GROUP, :], keys_by_queries[:, cols])
        for h in range(per_tile):
            parts.append(both[h * width : (h + 1) * width, h * GROUP : (h + 1) * GROUP])
    return jnp.concatenate(parts, axis=0)


def others(axis, size):
    me = lax.axis_index(axis)
    return [lax.rem(me + k, size) for k in range(1, size)]


def aligned(start, size):
    return pl.ds(pl.multiple_of(start, size), size)


def layer_kernel(
    parts, dp, length,
    nb_ref, x_hbm, up_hbm, tw_hbm, cw_hbm,
    out_hbm, sgrad_hbm, tg_ref, cg_ref,
    tw_ref, cw_ref, x_s, up_raw, up_s, stream_s, cols_s, sg_s, ret_s,
    t_nT, t_q, t_k, t_kT, t_v, t_iq, t_ik, t_w, t_mT, t_sg, back_s,
    c_q, c_k, c_v, c_g, c_kT, c_vT, c_iq, c_ik, c_dq, c_dk, c_dv, c_m, c_mT, c_nT,
    qbd, gbd, tile_keep, acc_s, all_s, core_in, chip_s, dp_in, mp_mine, mp_in, done_s, done_in,
    w_sem, x_sem, up_sem, out_sem, grad_sem, in_send, in_recv, back_send, back_recv, last_send, last_recv,
    send0, recv0, send1, recv1, send2, recv2, send3, recv3,
):
    segments, channels, features = up_s.shape
    own = stream_s.shape[1]
    rows_total = x_s.shape[0]
    chunks = rows_total // TIME_ROWS
    per_chunk = TIME_ROWS // length
    groups = TIME_ROWS // GROUP
    blocks_n, near = nb_ref.shape
    block = channels // blocks_n
    slots = qbd.shape[0]
    me = lax.axis_index("mp")
    me_dp = lax.axis_index("dp")
    peers = others("mp", parts)
    if parts == 4:
        peers = [lax.rem(me + 2, 4), 3 - me, me + 1 - 2 * lax.rem(me, 2)]
    dp_peers = others("dp", dp)

    def load_x(t):
        return pltpu.make_async_copy(
            x_hbm.at[aligned(t * TIME_ROWS, TIME_ROWS)], x_s.at[aligned(t * TIME_ROWS, TIME_ROWS)], x_sem.at[t]
        )

    def load_up():
        return pltpu.make_async_copy(up_hbm, up_raw, up_sem)

    load_weights = [
        pltpu.make_async_copy(tw_hbm, tw_ref, w_sem.at[0]),
        pltpu.make_async_copy(cw_hbm, cw_ref, w_sem.at[1]),
    ]
    load_x(0).start()
    load_weights[0].start()
    for t in range(1, chunks):
        load_x(t).start()
    load_weights[1].start()
    load_up().start()

    barrier = pltpu.get_barrier_semaphore()
    for peer in peers:
        pl.semaphore_signal(barrier, inc=1, device_id={"mp": peer}, device_id_type=MESH)
    for peer in dp_peers:
        pl.semaphore_signal(barrier, inc=1, device_id={"dp": peer}, device_id_type=MESH)

    blocks = head_blocks(features)
    cg = PERM_ROWS // length
    perm_t = regroup(cg, length)
    perm_tb = regroup(length, cg)
    tiles = features // GROUP
    sg_group = PERM_ROWS // (tiles * segments)
    qbd[...] = jnp.zeros_like(qbd)
    gbd[...] = jnp.zeros_like(gbd)
    tile_keep[...] = jnp.where(
        iota((GROUP, GROUP), 0) // length == iota((GROUP, GROUP), 1) // length, 1.0, 0.0
    ).astype(F32)
    c_dk[blocks_n * near] = jnp.zeros((block, features), F32)
    c_dv[blocks_n * near] = jnp.zeros((block, features), F32)

    load_weights[0].wait()

    def inward(k, seg):
        return pltpu.make_async_remote_copy(
            src_ref=stream_s.at[peers[k] * segments + seg],
            dst_ref=cols_s.at[seg, aligned(me * own, own)],
            send_sem=in_send.at[k, seg],
            recv_sem=in_recv.at[k, seg],
            device_id={"mp": peers[k]},
            device_id_type=MESH,
        )

    def inward_part(k, seg, t):
        return pltpu.make_async_remote_copy(
            src_ref=stream_s.at[peers[k] * segments + seg, aligned(t * per_chunk, per_chunk)],
            dst_ref=cols_s.at[seg, aligned(me * own + t * per_chunk, per_chunk)],
            send_sem=in_send.at[k, seg],
            recv_sem=in_recv.at[k, seg],
            device_id={"mp": peers[k]},
            device_id_type=MESH,
        )

    def back(k, seg):
        return pltpu.make_async_remote_copy(
            src_ref=sg_s.at[seg, aligned(peers[k] * own, own)],
            dst_ref=ret_s.at[me * segments + seg],
            send_sem=back_send.at[k, seg],
            recv_sem=back_recv.at[k, seg],
            device_id={"mp": peers[k]},
            device_id_type=MESH,
        )

    late = min(2, segments)
    first_late = segments - late

    def back_part(k, n, t):
        seg = first_late + n
        return pltpu.make_async_remote_copy(
            src_ref=sg_s.at[seg, aligned(peers[k] * own + t * per_chunk, per_chunk)],
            dst_ref=ret_s.at[me * segments + seg, aligned(t * per_chunk, per_chunk)],
            send_sem=last_send.at[k, n, t],
            recv_sem=last_recv.at[k, n, t],
            device_id={"mp": peers[k]},
            device_id_type=MESH,
        )

    half = per_chunk // 2

    def back_half(k, n, h):
        seg = first_late + n
        start = (chunks - 1) * per_chunk + h * half
        return pltpu.make_async_remote_copy(
            src_ref=sg_s.at[seg, aligned(peers[k] * own + start, half)],
            dst_ref=ret_s.at[me * segments + seg, pl.ds(start, half)],
            send_sem=last_send.at[k, n, chunks - 1 + h],
            recv_sem=last_recv.at[k, n, chunks - 1 + h],
            device_id={"mp": peers[k]},
            device_id_type=MESH,
        )

    def time_forward(t, carry):
        load_x(t).wait()
        rows = aligned(t * TIME_ROWS, TIME_ROWS)
        x = x_s[rows, :].astype(F32)
        normed = (x * inv_rms(x)).astype(BF16)
        t_nT[t] = normed.T
        q, iq = head_hat(mm(normed, tw_ref[0]), blocks)
        k, ik = head_hat(mm(normed, tw_ref[1]), blocks)
        v = mm(normed, tw_ref[2]).astype(BF16)
        t_q[rows, :], t_k[rows, :], t_v[rows, :] = q, k, v
        t_iq[rows, :], t_ik[rows, :] = iq, ik
        t_kT[t] = k.T
        vT = v.T
        keep = jnp.concatenate([tile_keep[...]] * HEADS, axis=1)
        mixed = []
        for g in range(groups):
            sl = slice(g * GROUP, (g + 1) * GROUP)
            bd = qbd.at[g % slots]
            fill_heads(bd, q[sl])
            e = jnp.exp2(EXP2_SCALE * mm_nt(k[sl], bd[...])) * keep
            w = (e * (1.0 / jnp.sum(e, axis=0, keepdims=True))).astype(BF16)
            t_w[t * groups + g] = w
            mT = head_product(vT[:, sl], w).astype(BF16)
            t_mT[t, :, sl] = mT
            mixed.append(mT.T)
        stream = (x + mm(jnp.concatenate(mixed, axis=0), tw_ref[3])).astype(BF16)
        for part in range(TIME_ROWS // PERM_ROWS):
            ordered = mm(perm_t, stream[part * PERM_ROWS : (part + 1) * PERM_ROWS]).astype(BF16)
            for seg in range(length):
                stream_s[seg, aligned(t * per_chunk + part * cg, cg), :] = ordered[seg * cg : (seg + 1) * cg]
        @pl.when(t == 0)
        def _():
            pl.semaphore_wait(barrier, len(peers) + len(dp_peers))

        for peer in range(parts - 1):
            inward_part(peer, 0, t).start()
        if segments > 1:

            @pl.when(t < chunks // 2)
            def _():
                for peer in range(parts - 1):
                    inward_part(peer, 1, t).start()

        return carry

    lax.fori_loop(0, chunks, time_forward, 0)
    for seg in range(1, segments):
        for k in range(parts - 1):
            if seg == 1:
                for t in range(chunks // 2, chunks):
                    inward_part(k, seg, t).start()
            else:
                inward(k, seg).start()
    for seg in range(segments):
        cols_s[seg, aligned(me * own, own), :] = stream_s[me * segments + seg]

    load_up().wait()
    load_weights[1].wait()
    perm_u = regroup(sg_group, tiles * segments)
    perm_ub = regroup(tiles * segments, sg_group)

    def order_up(pair, carry):
        both = [up_raw[aligned((pair * 2 + n) * PERM_ROWS, PERM_ROWS), :] for n in range(2)]
        ordered = mm(perm_u, jnp.concatenate(both, axis=1)).astype(BF16)
        for n in range(2):
            for tile in range(tiles):
                for seg in range(segments):
                    at = (tile * segments + seg) * sg_group
                    up_s[seg, aligned((pair * 2 + n) * sg_group, sg_group), tile * GROUP : (tile + 1) * GROUP] = ordered[
                        at : at + sg_group, n * GROUP : (n + 1) * GROUP
                    ]
        return carry

    lax.fori_loop(0, channels // (2 * sg_group), order_up, 0, unroll=True)

    row_step = min(channels, 512)
    step_blocks = row_step // block

    def one_segment(seg, carry):
        for k in range(parts - 1):
            inward(k, seg).wait_recv()

        def project(r, inner):
            rows = aligned(r * row_step, row_step)
            these = pl.ds(r * step_blocks, step_blocks)
            x = cols_s[seg, rows, :].astype(F32)
            normed = (x * inv_rms(x)).astype(BF16)
            c_nT[seg, r] = normed.T
            q, iq = head_hat(mm(normed, cw_ref[0]), blocks)
            k, ik = head_hat(mm(normed, cw_ref[1]), blocks)
            v = mm(normed, cw_ref[2]).astype(BF16)
            shaped = (step_blocks, block, features)
            c_q[these], c_k[these], c_v[these] = q.reshape(shaped), k.reshape(shaped), v.reshape(shaped)
            c_iq[these], c_ik[these] = iq.reshape(shaped), ik.reshape(shaped)
            kT = k.T
            vT = v.T
            for b in range(step_blocks):
                c_kT[r * step_blocks + b] = kT[:, b * block : (b + 1) * block]
                c_vT[r * step_blocks + b] = vT[:, b * block : (b + 1) * block]
            c_g[these] = mm_nt(up_s[seg, rows, :], cw_ref[3]).astype(BF16).reshape(shaped)
            return inner

        lax.fori_loop(0, channels // row_step, project, 0)

        def attend(pair, inner):
            for slot in range(slots):
                i = pair * slots + slot
                ids = [nb_ref[i, n] for n in range(near)]
                bd, gd = qbd.at[slot], gbd.at[slot]
                fill_heads(bd, c_q[i])
                fill_heads(gd, c_g[i])
                k_near = jnp.concatenate([c_k[j] for j in ids], axis=0)
                v_near = jnp.concatenate([c_v[j] for j in ids], axis=0)
                kT_near = jnp.concatenate([c_kT[j] for j in ids], axis=1)
                vT_near = jnp.concatenate([c_vT[j] for j in ids], axis=1)
                e = jnp.exp2(EXP2_SCALE * mm_nt(k_near, bd[...]))
                w = e * (1.0 / jnp.sum(e, axis=0, keepdims=True))
                w_b = w.astype(BF16)
                grad = mm_nt(v_near, gd[...])
                delta = jnp.sum(w * grad, axis=0, keepdims=True)
                t_b = (w * (grad - delta)).astype(BF16)
                mT = head_product(vT_near, w_b).astype(BF16)
                c_mT[seg, i] = mT
                c_m[seg, aligned(i * block, block), :] = mT.T
                dqT = (LOGIT_SCALE * head_product(kT_near, t_b)).astype(BF16)
                c_dq[i] = dqT.T
                c_dk[pl.ds(i * near, near)] = mm(t_b, bd[...]).reshape(near, block, features)
                c_dv[pl.ds(i * near, near)] = mm(w_b, gd[...]).reshape(near, block, features)
            return inner

        lax.fori_loop(0, blocks_n // slots, attend, 0)

        def finish_block(j):
            def place(i):
                at = blocks_n * near
                for n in range(1, near):
                    at = jnp.where(nb_ref[i, n] == j, i * near + n, at)
                return at

            def more(m, sums):
                at = place(lax.rem(j + m, blocks_n))
                return sums[0] + c_dk[at], sums[1] + c_dv[at]

            sums = (c_dk[j * near], c_dv[j * near])
            if blocks_n <= 4:
                for m in range(1, blocks_n):
                    sums = more(m, sums)
            else:
                sums = lax.fori_loop(1, blocks_n, more, sums)
            rows = aligned(j * block, block)
            qb = head_back(c_q[j], c_iq[j], c_dq[j].astype(F32), blocks)
            kb = head_back(c_k[j], c_ik[j], LOGIT_SCALE * sums[0], blocks)
            vb = sums[1].astype(BF16)
            at_rows = aligned(seg * channels + j * block, block)
            back_s[0, at_rows, :] = qb
            back_s[1, at_rows, :] = kb
            back_s[2, at_rows, :] = vb
            grad = mm_nt(qb, cw_ref[0]) + mm_nt(kb, cw_ref[1]) + mm_nt(vb, cw_ref[2])
            x = cols_s[seg, rows, :].astype(F32)
            sg_s[seg, rows, :] = (up_s[seg, rows, :].astype(F32) + row_back(x, grad)).astype(BF16)

        def finish(group, inner):
            for n in range(slots):
                finish_block(group * slots + n)
            return inner

        lax.fori_loop(0, blocks_n // slots, finish, 0)

        @pl.when(seg < first_late)
        def _():
            for k in range(parts - 1):
                back(k, seg).start()

        if late > 1:

            @pl.when(seg == first_late)
            def _():
                for t in range(chunks // 4):
                    for k in range(parts - 1):
                        back_part(k, 0, t).start()

        ret_s[me * segments + seg] = sg_s[seg, aligned(me * own, own), :]
        return carry

    lax.fori_loop(0, segments, one_segment, 0)
    for t in range(chunks - 1):
        for n in range(late):
            if n < late - 1 and t < chunks // 4:
                continue
            for k in range(parts - 1):
                back_part(k, n, t).start()

    for h in range(2):
        for n in range(late):
            for k in range(parts - 1):
                back_half(k, n, h).start()

    matrices = tw_ref.shape[0]
    width = all_s.shape[4]
    core, chip = lax.rem(me_dp, 2), me_dp // 2
    chips = dp // 2
    chip_peers = [lax.rem(chip + k, chips) for k in range(1, chips)]
    splits = features // width

    def exchange(src, dst, send, recv, device):
        return pltpu.make_async_remote_copy(
            src_ref=src, dst_ref=dst, send_sem=send, recv_sem=recv, device_id=device, device_id_type=MESH
        )

    def put_grad(r, m, value):
        for part in range(splits):
            place = m * splits + part
            all_s[r, place % 2, place // 2] = value[:, part * width : (part + 1) * width].astype(BF16)

    def stage0(r):
        return [exchange(all_s.at[r, 1 - core], core_in.at[r], send0.at[r], recv0.at[r], {"dp": me_dp + 1 - 2 * core})]

    def stage1(r):
        return [
            exchange(chip_s.at[r, p], dp_in.at[r, k], send1.at[r, k], recv1.at[r, k], {"dp": p * 2 + core})
            for k, p in enumerate(chip_peers)
        ]

    def stage2(r):
        return [
            exchange(mp_mine.at[r, p], mp_in.at[r, k], send2.at[r, k], recv2.at[r, k], {"mp": p})
            for k, p in enumerate(peers)
        ]

    def stage3(r):
        return [
            exchange(done_s.at[r], done_in.at[r, me_dp], send3.at[r, k], recv3.at[r, k], {"dp": p})
            for k, p in enumerate(dp_peers)
        ]

    def start(copies):
        for copy in copies:
            copy.start()

    def wait(copies):
        for copy in copies:
            copy.wait()

    def finish0(r):
        wait(stage0(r))
        chip_s[r] = (all_s[r, core].astype(F32) + core_in[r].astype(F32)).astype(BF16)
        start(stage1(r))

    def finish1(r):
        wait(stage1(r))
        total = chip_s[r, chip].astype(F32)
        for k in range(chips - 1):
            total = total + dp_in[r, k].astype(F32)
        mp_mine[r] = total.astype(BF16).reshape(mp_mine.shape[1:])
        start(stage2(r))

    def finish2(r):
        wait(stage2(r))
        total = mp_mine[r, me].astype(F32)
        for k in range(parts - 1):
            total = total + mp_in[r, k].astype(F32)
        done_s[r] = total.astype(BF16)
        start(stage3(r))
        done_in[r, me_dp] = done_s[r]

    def finish3(r, ref):
        wait(stage3(r))
        for m in range(matrices):
            for part in range(splits):
                ref[m, :, part * width : (part + 1) * width] = done_in[r, m * splits + part].astype(F32) / dp

    steps = channels // row_step
    for m in range(matrices):
        total = None
        for seg in range(segments):
            for r in range(steps):
                rows = slice(r * row_step, (r + 1) * row_step)
                if m < 3:
                    term = mm(c_nT[seg, r], back_s[m, seg * channels + r * row_step : seg * channels + (r + 1) * row_step, :])
                else:
                    mT = jnp.concatenate([c_mT[seg, r * step_blocks + b] for b in range(step_blocks)], axis=1)
                    term = mm(mT, up_s[seg, rows, :])
                total = term if total is None else total + term
        put_grad(1, m, total)
    start(stage0(1))


    def project_out(r, carry):
        rows = aligned(r * row_step, row_step)
        for seg in range(segments):
            res = cols_s[seg, rows, :].astype(F32) + mm(c_m[seg, rows, :], cw_ref[3])
            c_m[seg, rows, :] = res.astype(BF16)
        return carry

    def order_out(pair, carry):
        both = []
        for n in range(2):
            rows = aligned((pair * 2 + n) * sg_group, sg_group)
            both.append(
                jnp.concatenate(
                    [
                        c_m[seg, rows, tile * GROUP : (tile + 1) * GROUP]
                        for tile in range(tiles)
                        for seg in range(segments)
                    ],
                    axis=0,
                )
            )
        ordered = mm(perm_ub, jnp.concatenate(both, axis=1)).astype(BF16)
        for n in range(2):
            up_raw[aligned((pair * 2 + n) * PERM_ROWS, PERM_ROWS), :] = ordered[:, n * GROUP : (n + 1) * GROUP]
        return carry

    out_copy = pltpu.make_async_copy(up_raw, out_hbm, out_sem)

    lax.fori_loop(0, channels // row_step, project_out, 0)
    lax.fori_loop(0, channels // (2 * sg_group), order_out, 0, unroll=True)
    out_copy.start()
    finish0(1)
    for seg in range(first_late):
        for k in range(parts - 1):
            back(k, seg).wait_recv()

    def backward_rows(t, off, size):
        rows = aligned(t * TIME_ROWS + off, size)
        ordered = []
        for part in range(size // PERM_ROWS):
            at = aligned(t * per_chunk + off // length + part * cg, cg)
            slabs = jnp.concatenate([ret_s[seg, at, :] for seg in range(length)], axis=0)
            ordered.append(mm(perm_tb, slabs).astype(BF16))
        up_b = jnp.concatenate(ordered, axis=0)
        t_sg[rows, :] = up_b
        mg = mm_nt(up_b, tw_ref[3]).astype(BF16)
        q, k, v = t_q[rows, :], t_k[rows, :], t_v[rows, :]
        kT = t_kT[t, :, off : off + size]
        dq, dk, dv = [], [], []
        for g in range(size // GROUP):
            sl = slice(g * GROUP, (g + 1) * GROUP)
            bd, gd = qbd.at[g % slots], gbd.at[g % slots]
            fill_heads(bd, q[sl])
            fill_heads(gd, mg[sl])
            w_b = t_w[t * groups + off // GROUP + g]
            w = w_b.astype(F32)
            grad = mm_nt(v[sl], gd[...])
            delta = jnp.sum(w * grad, axis=0, keepdims=True)
            t_b = (w * (grad - delta)).astype(BF16)
            dqT = (LOGIT_SCALE * head_product(kT[:, sl], t_b)).astype(BF16)
            dq.append(dqT.T.astype(F32))
            dk.append(LOGIT_SCALE * mm(t_b, bd[...]))
            dv.append(mm(w_b, gd[...]).astype(BF16))
        qb = head_back(q, t_iq[rows, :], jnp.concatenate(dq, axis=0), blocks)
        kb = head_back(k, t_ik[rows, :], jnp.concatenate(dk, axis=0), blocks)
        vb = jnp.concatenate(dv, axis=0)
        back_s[0, rows, :] = qb
        back_s[1, rows, :] = kb
        back_s[2, rows, :] = vb
        nT = t_nT[t, :, off : off + size]
        first = t == 0
        for m, back_rows in enumerate((qb, kb, vb)):
            acc_s[m] = mm(nT, back_rows) + jnp.where(first, 0.0, acc_s[m])
        acc_s[3] = mm(t_mT[t, :, off : off + size], up_b) + jnp.where(first, 0.0, acc_s[3])

    def time_backward(t, carry):
        for n in range(late):
            for k in range(parts - 1):
                back_part(k, n, t).wait_recv()
        backward_rows(t, 0, TIME_ROWS)
        pl.when(t == 0)(functools.partial(finish1, 1))
        return carry

    acc_s[...] = jnp.zeros_like(acc_s)
    lax.fori_loop(0, chunks - 1, time_backward, 0)
    for h in range(2):
        for n in range(late):
            for k in range(parts - 1):
                back_half(k, n, h).wait_recv()
        backward_rows(chunks - 1, h * (TIME_ROWS // 2), TIME_ROWS // 2)
    for m in range(matrices):
        put_grad(0, m, acc_s[m])
    start(stage0(0))

    def series_back(t, carry):
        rows = aligned(t * TIME_ROWS, TIME_ROWS)
        grad = mm_nt(back_s[0, rows, :], tw_ref[0]) + mm_nt(back_s[1, rows, :], tw_ref[1])
        grad = grad + mm_nt(back_s[2, rows, :], tw_ref[2])
        x = x_s[rows, :].astype(F32)
        t_sg[rows, :] = (t_sg[rows, :].astype(F32) + row_back(x, grad)).astype(BF16)
        return carry

    lax.fori_loop(0, chunks // 4, series_back, 0)
    finish0(0)
    finish2(1)
    lax.fori_loop(chunks // 4, chunks, series_back, 0)
    finish1(0)
    grad_copy = pltpu.make_async_copy(t_sg, sgrad_hbm, grad_sem)
    grad_copy.start()
    finish3(1, cg_ref)
    finish2(0)
    finish3(0, tg_ref)

    grad_copy.wait()
    out_copy.wait()
    for k in range(parts - 1):
        for seg in range(segments):
            inward(k, seg).wait_send()
        for seg in range(first_late):
            back(k, seg).wait_send()
        for n in range(late):
            for t in range(chunks - 1):
                back_part(k, n, t).wait_send()
            for h in range(2):
                back_half(k, n, h).wait_send()


SETTLE_PARTS = 2


def settle_kernel(count, *refs):
    sources, results, held = refs[:count], refs[count : 2 * count], refs[2 * count : 3 * count]
    in_sem, out_sem = refs[3 * count :]
    loads, stores = [], []
    for n in range(count):
        step = held[n].shape[0] // SETTLE_PARTS
        for part in range(SETTLE_PARTS):
            rows = pl.ds(part * step, step)
            loads.append(pltpu.make_async_copy(sources[n].at[rows], held[n].at[rows], in_sem.at[n, part]))
            stores.append(pltpu.make_async_copy(held[n].at[rows], results[n].at[rows], out_sem.at[n, part]))
    for load in loads:
        load.start()
    for load, store in zip(loads, stores):
        load.wait()
        store.start()
    for store in stores:
        store.wait()


def settle(*arrays):
    count = len(arrays)
    hbm = pl.BlockSpec(memory_space=pl.ANY)
    return pl.pallas_call(
        functools.partial(settle_kernel, count),
        out_shape=tuple(jax.ShapeDtypeStruct(a.shape, a.dtype) for a in arrays),
        in_specs=[hbm] * count,
        out_specs=(hbm,) * count,
        scratch_shapes=[pltpu.VMEM(a.shape, a.dtype) for a in arrays]
        + [pltpu.SemaphoreType.DMA((count, SETTLE_PARTS))] * 2,
        name="settle",
    )(*arrays)


VMEM_LIMIT = 62 * 1024 * 1024


def shards(series, upstream_grad, time_weights, channel_weights, neighbors):
    parts, dp = lax.axis_size("mp"), lax.axis_size("dp")
    own, length, features = series.shape[1:]
    channels, segments = upstream_grad.shape[1:3]
    blocks_n, near = neighbors.shape
    block = channels // blocks_n
    matrices = time_weights.shape[0]
    total = own * length
    chunks = total // TIME_ROWS
    row_step = min(channels, 512)
    steps = channels // row_step
    slots = 4 if blocks_n <= 4 else 2
    mine = features // parts
    width = features * matrices // dp
    tiles = features // GROUP
    upstream = jnp.swapaxes(upstream_grad.reshape(channels, segments, tiles, GROUP), 1, 2)
    vmem = pl.BlockSpec(memory_space=pltpu.VMEM)
    hbm = pl.BlockSpec(memory_space=pl.ANY)
    dma = lambda *shape: pltpu.SemaphoreType.DMA(shape)
    b16 = lambda *shape: pltpu.VMEM(shape, BF16)
    f32 = lambda *shape: pltpu.VMEM(shape, F32)
    grads = jax.ShapeDtypeStruct((matrices, mine, features), F32)
    per_block = (blocks_n, block, features)
    contributions = f32(blocks_n * near + 1, block, features)
    output, series_grad, time_grads, channel_grads = pl.pallas_call(
        functools.partial(layer_kernel, parts, dp, length),
        out_shape=(
            jax.ShapeDtypeStruct((channels * segments * tiles, GROUP), BF16),
            jax.ShapeDtypeStruct((total, features), BF16),
            grads,
            grads,
        ),
        in_specs=[pl.BlockSpec(memory_space=pltpu.SMEM), hbm, hbm, hbm, hbm],
        out_specs=(hbm, hbm, vmem, vmem),
        scratch_shapes=[
            b16(*time_weights.shape),
            b16(*channel_weights.shape),
            b16(total, features),
            b16(channels * segments * tiles, GROUP),
            b16(segments, channels, features),
            b16(length, own, features),
            b16(segments, channels, features),
            b16(segments, channels, features),
            b16(length, own, features),
            b16(chunks, features, TIME_ROWS),
            b16(total, features),
            b16(total, features),
            b16(chunks, features, TIME_ROWS),
            b16(total, features),
            f32(total, features),
            f32(total, features),
            b16(total // GROUP, GROUP, HEADS * GROUP),
            b16(chunks, features, TIME_ROWS),
            b16(total, features),
            b16(3, total, features),
            b16(*per_block),
            b16(*per_block),
            b16(*per_block),
            b16(*per_block),
            b16(blocks_n, features, block),
            b16(blocks_n, features, block),
            f32(*per_block),
            f32(*per_block),
            b16(*per_block),
            contributions,
            contributions,
            b16(segments, channels, features),
            b16(segments, blocks_n, features, block),
            b16(segments, steps, features, row_step),
            b16(slots, HEADS * GROUP, features),
            b16(slots, HEADS * GROUP, features),
            f32(GROUP, GROUP),
            f32(matrices, features, features),
            b16(2, 2, dp // 2, features, width),
            b16(2, dp // 2, features, width),
            b16(2, dp // 2, features, width),
            b16(2, dp // 2 - 1, features, width),
            b16(2, parts, mine, width),
            b16(2, parts - 1, mine, width),
            b16(2, mine, width),
            b16(2, dp, mine, width),
            dma(2), dma(chunks), pltpu.SemaphoreType.DMA, pltpu.SemaphoreType.DMA, pltpu.SemaphoreType.DMA,
            dma(parts - 1, segments), dma(parts - 1, segments),
            dma(parts - 1, segments), dma(parts - 1, segments),
            dma(parts - 1, min(2, segments), chunks + 1), dma(parts - 1, min(2, segments), chunks + 1),
            dma(2), dma(2), dma(2, dp // 2 - 1), dma(2, dp // 2 - 1), dma(2, parts - 1), dma(2, parts - 1), dma(2, dp - 1), dma(2, dp - 1),
        ],
        compiler_params=pltpu.CompilerParams(
            vmem_limit_bytes=VMEM_LIMIT, collective_id=0, has_side_effects=True
        ),
        name="layer",
    )(
        neighbors,
        series.reshape(total, features),
        upstream.reshape(channels * segments * tiles, GROUP),
        time_weights,
        channel_weights,
    )
    output, series_grad, time_grads, channel_grads = settle(output, series_grad, time_grads, channel_grads)
    output = jnp.swapaxes(output.reshape(channels, tiles, segments, GROUP), 1, 2)
    return (
        output.reshape(upstream_grad.shape),
        series_grad.reshape(series.shape),
        time_grads,
        channel_grads,
    )


def solution(mesh):
    placed = (P("dp", "mp", None, None), P("dp", None, "mp", None), P(), P(), P())
    return jax.shard_map(
        shards,
        mesh=mesh,
        in_specs=placed,
        out_specs=(
            P("dp", None, "mp", None),
            P("dp", "mp", None, None),
            P(None, "mp", None),
            P(None, "mp", None),
        ),
        check_vma=False,
    )
```
